256 devices in a mesh: pipe: 4 (over y), rows: 64 (over x, z, core).
Axes of the slice: x: 4, y: 4, z: 8, core: 2. Of those that a mesh axis runs over, the one named last changes fastest.
Arguments:
- features: bfloat16 [128, 65536], P('pipe', 'rows'), may hold values from 0 to 16
- weights: bfloat16 [8, 1024, 64, 256], P('pipe', 'rows'), may hold values from -0.5 to 0.5
- bias: bfloat16 [8, 65536], P('pipe', 'rows'), may hold values from -2 to 2
- layout: int32 [8, 4096], P('pipe'), may hold values from 0 to 1023, as said below
Outputs:
- activations: bfloat16 [128, 65536], P('pipe', 'rows')
The draws below stay inside these ranges and needn't reach their ends.
Inputs may be any that keep to these rules, and one draw needn't show every extreme that they name: `layout`: for every layer and every index of rows, the 64 slots of that index's 16 output blocks read blocks held by exactly 32 distinct indices of rows (index = block // 16), exactly 2 slots from each of them.
All inputs are finite; a program needn't handle non-finite values.
Results may differ from the reference program's by a relative error of at most 0.013.
Values may be sent and summed in bfloat16 or wider, within the bound.
A program may use at most 64 MiB of HBM per device.

```python
import jax
import jax.numpy as jnp
from jax import lax

NEURONS = 65536
BLOCK = 64
K = 4
LAYERS = 8
BATCH = 128
NB = 1024
BD = 16
SLOTS = 64
GROUPS = 32
N_ROWS = 64


def draw_layout(key, part):

    def one_group(inner_key):
        first_key, second_key, third_key = jax.random.split(inner_key, 3)
        owners = jax.random.permutation(first_key, N_ROWS)[:GROUPS]
        ordering = jax.random.permutation(second_key, SLOTS)
        sources = owners[ordering % GROUPS]
        locals_drawn = jax.random.randint(third_key, (SLOTS,), 0, BD)
        return (sources * BD + locals_drawn).astype(jnp.int32)
    all_keys = jax.random.split(jax.random.fold_in(key, 7), LAYERS * N_ROWS)
    return jax.vmap(one_group)(all_keys).reshape(LAYERS, NB * K)


def shard_levels(rng, dims, pieces, smallest, top_value):
    loudness, own = 1.0, jax.random.fold_in(rng, 6)
    for position, blocks in pieces:
        heights = jnp.exp(jax.random.uniform(jax.random.fold_in(own, position), (blocks,), jnp.float32, smallest / len(pieces), top_value / len(pieces)))
        loudness = loudness * jnp.repeat(heights, dims[position] // blocks).reshape([-1 if axis == position else 1 for axis in range(len(dims))])
    return loudness


def normal_values(key, dims, width, bound, shards=(), held_as=jnp.bfloat16):
    array = jax.random.normal(key, dims, jnp.float32) * width
    if len(shards) > 0:
        array = shard_levels(key, dims, shards, -0.22, 0.18) * array
    return jnp.clip(array, min=-bound, max=bound).astype(held_as)


def setup_inputs(seed: int = 0) -> dict:
    splits = jax.random.split(jax.random.key(seed), 5)
    return {
        "features": jnp.clip(16.0 * jax.random.uniform(splits[0], (BATCH, NEURONS), jnp.float32) ** shard_levels(splits[0], (BATCH, NEURONS), ((0, 4), (1, 64)), -0.2, 0.2), 0.0, 16.0).astype(jnp.bfloat16),
        "weights": normal_values(splits[1], (LAYERS, NB, BLOCK, K * BLOCK), (K * BLOCK // 2) ** -0.5, 0.5, ((0, 4), (1, 64))),
        "bias": jnp.clip(jax.random.uniform(splits[2], (LAYERS, NEURONS), jnp.float32, -2.0, 2.0) * shard_levels(splits[2], (LAYERS, NEURONS), ((0, 4), (1, 64)), -0.4, 0.0), -2.0, 2.0).astype(jnp.bfloat16),
        "layout": draw_layout(jax.random.fold_in(splits[4], 71), 0),
    }


clamp_top = 32.0
span_blocks = 16


def reference(features, weights, bias, layout):
    current = features.reshape(BATCH, NB, BLOCK)
    for layer_idx in range(LAYERS):
        index_parts = layout[layer_idx].reshape(NB // span_blocks, span_blocks * K)
        reordered = jnp.transpose(weights[layer_idx].reshape(NB, BLOCK, K, BLOCK), (0, 2, 1, 3))
        weight_parts = reordered.reshape(NB // span_blocks, span_blocks * K, BLOCK, BLOCK)

        def one_span(pair):
            indices, weight_span = pair
            inputs = jnp.take(current, indices, axis=1).astype(jnp.float32)
            products = jnp.einsum('rsf,sfg->rsg', inputs, weight_span.astype(jnp.float32))
            return products.reshape(BATCH, span_blocks, K, BLOCK).sum(axis=2)

        spans = lax.map(one_span, (index_parts, weight_parts))
        summed = jnp.transpose(spans, (1, 0, 2, 3)).reshape(BATCH, NB * BLOCK)
        summed = summed + bias[layer_idx].astype(jnp.float32)[None, :]
        current = jnp.clip(jax.nn.relu(summed), 0.0, clamp_top).astype(jnp.bfloat16).reshape(BATCH, NB, BLOCK)
    return current.reshape(BATCH, NEURONS)
```

```python
import functools

import jax
import jax.numpy as jnp
from jax import lax
from jax.experimental import pallas as pl
from jax.experimental.pallas import tpu as pltpu
from jax.sharding import PartitionSpec as P

MESH = pl.DeviceIdType.MESH
BLOCK = 64
K = 4
X, Z, C = 4, 8, 2
PIPE = 4
ROWS = X * Z * C
LAYERS = 8
OWN = LAYERS // PIPE
BD = 16
SUBS = 2
CHUNKS = 4
clamp_top = 32.0

NEAR, AHEAD, BACK, FAR = (0, 6), (6, 4), (10, 4), (14, 2)


def place():
    me = lax.axis_index("rows")
    return lax.axis_index("pipe"), me // (Z * C), (me // C) % Z, me % C


def device(dy, dx, dz, dc):
    y, x, z, c = place()
    row = (((x + dx + X) % X) * Z + (z + dz + Z) % Z) * C + (c + dc) % C
    return ((y + dy + PIPE) % PIPE, row)


def offsets():
    found = [(1, 0, 0, 0), (2, 0, 0, 0), (3, 0, 0, 0), (0, 0, 2, 0), (0, 0, -2, 0)]
    for dx in range(X):
        for dc in range(C):
            for dz in (0, 1, -1, 2 if dc == 0 else -2):
                here = (0, dx, dz, dc)
                if here not in found and here != (0, 0, 0, 0):
                    found.append(here)
    return found


def swap_halves(v):
    return pltpu.roll(v, BLOCK, 1)


def kernel(
    feat_ref, w_hbm, bias_ref, lay_ref, out_ref,
    wall, ready, biases, bias_tiles, tabs, stab, cur, stage, land,
    local_sem, tab_send, tab_recv, bias_send, bias_recv, w_send, w_recv,
    hop_send, hop_recv, leaf_send, leaf_recv,
):
    y, x, z, c = place()
    me = (x * Z + z) * C + c
    rs = cur[0][0].shape[2]
    left = lax.broadcasted_iota(jnp.int32, (BD, 128), 1) < BLOCK

    barrier = pltpu.get_barrier_semaphore()
    partners = offsets()
    for dy, dx, dz, dc in partners:
        pl.semaphore_signal(
            barrier, inc=1, device_id=device(-dy, -dx, -dz, -dc), device_id_type=MESH
        )

    own_w = pltpu.make_async_copy(w_hbm, wall.at[pl.ds(OWN * y, OWN)], local_sem.at[0])
    own_w.start()

    def fold(p, carry):
        cols = pl.ds(pl.multiple_of(p * 128, 128), 128)
        low = feat_ref[pl.ds(0, 16), cols].astype(jnp.float32)
        high = feat_ref[pl.ds(16, 16), cols].astype(jnp.float32)
        even = jnp.where(left, low, swap_halves(high)).astype(jnp.bfloat16)
        odd = jnp.where(left, swap_halves(low), high).astype(jnp.bfloat16)
        for s in range(SUBS):
            cur[0][s][0, 2 * p] = even[s * rs : (s + 1) * rs]
            cur[0][s][0, 2 * p + 1] = odd[s * rs : (s + 1) * rs]
        return carry

    lax.fori_loop(0, BD // 2, fold, 0)
    biases[pl.ds(y, 1)] = bias_ref[...].reshape(1, OWN, bias_ref.shape[1])

    lane = lax.broadcasted_iota(jnp.int32, (ROWS // 2, 128), 1)
    slot = lane & 63
    for a in range(OWN):
        entry = lay_ref[a]
        owner = entry >> 4
        key = slot * BD + (entry & 15)
        table = jnp.zeros((ROWS // 2, 128), jnp.int32)
        for q, dz in enumerate((0, -2, 2)):
            source = (x * Z + (z + dz + Z) % Z) * C + c
            for half in range(2):
                hit = (owner == source) & ((lane >> 6) == half)
                first = jnp.min(jnp.where(hit, key, 1 << 20), axis=1, keepdims=True) & 15
                last = jnp.max(jnp.where(hit, key, 0), axis=1, keepdims=True) & 15
                table = jnp.where(lane == 4 * q + 2 * half, first, table)
                table = jnp.where(lane == 4 * q + 2 * half + 1, last, table)
        tabs[y, a, pl.ds(0, ROWS // 2)] = table
    mine = jnp.concatenate(
        [lay_ref[a, pl.ds(x * Z + z, 1), :] for a in range(OWN)]
        + [jnp.zeros((8 - OWN, 128), jnp.int32)],
        axis=0,
    )
    owner = mine >> 4
    spot = lax.broadcasted_iota(jnp.int32, (8, 128), 1) & 63
    rank = jnp.zeros((8, 128), jnp.int32)
    for step in range(1, 64):
        same = (pltpu.roll(owner, step, 1) == owner) & (spot >= step)
        rank = jnp.where(same, 1, rank)
    dx = (x - (owner >> 4) + X) & (X - 1)
    dz = (z - ((owner >> 1) & (Z - 1)) + Z) & (Z - 1)
    dc = (c + owner) & 1
    base = jnp.zeros((8, 128), jnp.int32)
    for d, at in ((0, 0), (2, 2), (6, 4), (1, 6), (3, 8), (7, 10), (5, 12), (4, 14)):
        base = jnp.where(dz == d, at, base)
    where = (dx * 2 + dc) * 16 + base + rank
    for a in range(OWN):
        tabs[y, a, pl.ds(ROWS // 2, 8)] = jnp.broadcast_to(where[a : a + 1], (8, 128))

    pl.semaphore_wait(barrier, len(partners))

    def tab_copy(dy):
        return pltpu.make_async_remote_copy(
            tabs.at[y], tabs.at[y], tab_send, tab_recv,
            device_id=device(dy, 0, 0, 0), device_id_type=MESH,
        )

    def bias_copy(dy):
        return pltpu.make_async_remote_copy(
            biases.at[y], biases.at[y], bias_send, bias_recv,
            device_id=device(dy, 0, 0, 0), device_id_type=MESH,
        )

    def hop(l, s, dz, q):
        return pltpu.make_async_remote_copy(
            cur[l][s].at[0], cur[l][s].at[q], hop_send.at[l, s], hop_recv.at[l, s],
            device_id=device(0, 0, dz, 0), device_id_type=MESH,
        )

    def start_hops(l, s):
        hop(l, s, 2, 1).start()
        hop(l, s, -2, 2).start()

    rows = BD // CHUNKS

    def w_copy(l, chunk, dy, src):
        piece = pl.ds(chunk * rows, rows)
        return pltpu.make_async_remote_copy(
            src.at[piece], wall.at[l, piece], w_send, w_recv.at[l, chunk],
            device_id=device(dy, 0, 0, 0), device_id_type=MESH,
        )

    def w_own(a, dy, order):
        for chunk in order:
            w_copy(OWN * y + a, chunk, dy, w_hbm.at[a]).start()

    def w_wait(l, order):
        for chunk in order:
            w_copy(l, chunk, 1, wall.at[l]).wait_recv()

    def w_pass(l, order, dy):
        for chunk in order:
            w_wait(l, (chunk,))
            w_copy(l, chunk, dy, wall.at[l]).start()

    def at_y(which, act):
        pl.when(y == which)(act)

    first_half, last_half, forward, turned = (0, 1), (2, 3), (0, 1, 2, 3), (2, 3, 0, 1)

    def point(p):
        if p == 0:
            @functools.partial(at_y, 0)
            def _():
                for a in range(OWN):
                    w_own(a, 1, forward)
                    w_own(a, -1, turned)

            @functools.partial(at_y, 1)
            def _():
                for a in range(OWN):
                    w_own(a, -1, turned)

        if p == 1:
            @functools.partial(at_y, 1)
            def _():
                w_pass(0, first_half, 1)
                w_own(0, 1, first_half)

            @functools.partial(at_y, 3)
            def _():
                w_pass(0, last_half, -1)

        if p == 2:
            @functools.partial(at_y, 1)
            def _():
                w_pass(1, first_half, 1)
                w_own(0, 1, last_half)
                w_own(1, 1, forward)

            @functools.partial(at_y, 3)
            def _():
                w_pass(1, last_half, -1)

            @functools.partial(at_y, 0)
            def _():
                w_pass(2, last_half, -1)
                w_pass(3, last_half, -1)

            @functools.partial(at_y, 2)
            def _():
                w_pass(2, first_half, 1)
                for dy in (1, 3, 2):
                    w_own(0, dy, forward)

        if p == 3:
            @functools.partial(at_y, 2)
            def _():
                w_pass(3, first_half, 1)
                for dy in (1, 3, 2):
                    w_own(1, dy, forward)

            @functools.partial(at_y, 3)
            def _():
                for a in range(OWN):
                    for dy in (1, 3, 2):
                        w_own(a, dy, forward)

    def arrive(l):
        own = l // OWN
        for who in range(PIPE):
            dist = (who - own) % PIPE
            order = forward
            if l < 4:
                order = {1: last_half, 2: forward, 3: first_half}.get(dist, ())
            if dist:
                at_y(who, functools.partial(w_wait, l, order))
        if l % OWN == 0:
            at_y(own, own_w.wait)

    def prepare(l):
        keep = lax.broadcasted_iota(jnp.int32, (BLOCK, 128), 1) < BLOCK

        def one(r, carry):
            for p in range(2):
                raw = wall[l, r, :, pl.ds(p * 128, 128)].astype(jnp.float32)
                turn = swap_halves(raw)
                zero = jnp.zeros_like(raw)
                parts = (
                    jnp.where(keep, raw, zero), jnp.where(keep, zero, turn),
                    jnp.where(keep, turn, zero), jnp.where(keep, zero, raw),
                )
                for i, part in enumerate(parts):
                    ready[l, r, pl.ds((p * 4 + i) * BLOCK, BLOCK), :] = part.astype(jnp.bfloat16)
            return carry

        lax.fori_loop(0, BD, one, 0)

        line_left = lax.broadcasted_iota(jnp.int32, (1, 128), 1) < BLOCK

        for p in range(BD // 2):
            row = biases[l // OWN, pl.ds(l % OWN, 1), pl.ds(p * 128, 128)].astype(jnp.float32)
            turn = swap_halves(row)
            bias_tiles[l, pl.ds(2 * p, 1), :] = jnp.where(line_left, row, turn)
            bias_tiles[l, pl.ds(2 * p + 1, 1), :] = jnp.where(line_left, turn, row)

    def leaf(l, s, u, dx, dz, dc, part):
        tiles = pl.ds(u * 16 + part[0], part[1])
        return pltpu.make_async_remote_copy(
            stage.at[l, s, tiles], land[l][s].at[tiles], leaf_send.at[l, s], leaf_recv.at[l, s],
            device_id=device(0, dx, dz, dc), device_id_type=MESH,
        )

    def spread(l, s):
        pltpu.make_async_remote_copy(
            cur[l][s].at[pl.ds(1, 2)], cur[l][s].at[pl.ds(1, 2)], hop_send.at[l, s], hop_recv.at[l, s],
            device_id=device(0, 0, 2, 0), device_id_type=MESH,
        ).wait_recv()

        def column(t, carry):
            dx = (t // 2) ^ 2
            dc = t % 2
            u = dx * 2 + dc
            cc = (c + dc) % C
            xx = ((x + dx) % X) * Z

            def put(at, q, dz):
                for k in range(2):
                    index = stab[l // OWN, l % OWN, xx + (z + dz + Z) % Z, 4 * q + 2 * cc + k]
                    stage[l, s, u * 16 + at + k] = cur[l][s][q, index]

            far = 2 - 4 * dc
            put(14, 1 + dc, far)
            leaf(l, s, u, dx, far, dc, FAR).start()
            put(6, 0, 1)
            put(8, 1, 1)
            leaf(l, s, u, dx, 1, dc, AHEAD).start()
            put(10, 0, -1)
            put(12, 2, -1)
            leaf(l, s, u, dx, -1, dc, BACK).start()
            put(0, 0, 0)
            put(2, 1, 0)
            put(4, 2, 0)

            @pl.when(u > 0)
            def _():
                leaf(l, s, u, dx, 0, dc, NEAR).start()

            return carry

        lax.fori_loop(0, X * C, column, 0)
        for k in range(NEAR[1]):
            land[l][s][k] = stage[l, s, k]

    def gather(l, s):
        tiles = pl.ds(NEAR[1], 8 * 16 - NEAR[1])
        pltpu.make_async_remote_copy(
            stage.at[l, s, tiles], land[l][s].at[tiles], leaf_send.at[l, s], leaf_recv.at[l, s],
            device_id=device(0, 1, 0, 0), device_id_type=MESH,
        ).wait_recv()

    def block_out(l, s, r):
        row = stab.at[l // OWN, l % OWN, ROWS // 2]
        lhs = jnp.concatenate([land[l][s][row[c * 64 + r * K + k]] for k in range(K)], axis=1)
        total = jnp.dot(lhs, ready[l, r], preferred_element_type=jnp.float32)
        total = total + bias_tiles[l, pl.ds(r, 1), :]
        return jnp.minimum(jnp.maximum(total, 0.0), clamp_top)

    def advance(l, s):
        gather(l, s)

        def pair(p, carry):
            for r in range(2):
                cur[l + 1][s][0, 2 * p + r] = block_out(l, s, 2 * p + r).astype(jnp.bfloat16)
            return carry

        lax.fori_loop(0, BD // 2, pair, 0)
        start_hops(l + 1, s)

    def finish(l, s):
        gather(l, s)
        half = left[:rs]

        def pair(p, carry):
            even, odd = block_out(l, s, 2 * p), block_out(l, s, 2 * p + 1)
            cols = pl.ds(pl.multiple_of(p * 128, 128), 128)
            low = jnp.where(half, even, swap_halves(odd))
            high = jnp.where(half, swap_halves(even), odd)
            out_ref[pl.ds(s * rs, rs), cols] = low.astype(jnp.bfloat16)
            out_ref[pl.ds(16 + s * rs, rs), cols] = high.astype(jnp.bfloat16)
            return carry

        lax.fori_loop(0, BD // 2, pair, 0)

    for dy in (2, 1, 3):
        tab_copy(dy).start()
    for s in range(SUBS):
        start_hops(0, s)
    for dy in (1, 2, 3):
        bias_copy(dy).start()
    point(0)
    pltpu.make_async_remote_copy(
        tabs.at[pl.ds(0, 3)], tabs.at[pl.ds(0, 3)], tab_send, tab_recv,
        device_id=device(1, 0, 0, 0), device_id_type=MESH,
    ).wait()
    to_smem = pltpu.make_async_copy(tabs, stab, local_sem.at[1])
    to_smem.start()
    to_smem.wait()

    last = LAYERS - 1
    spread(0, 0)
    spread(0, 1)
    point(1)
    pltpu.make_async_remote_copy(
        biases.at[pl.ds(0, 3)], biases.at[pl.ds(0, 3)], bias_send, bias_recv,
        device_id=device(1, 0, 0, 0), device_id_type=MESH,
    ).wait()
    arrive(0)
    prepare(0)
    for l in range(LAYERS):
        if l < last:
            advance(l, 0)
            spread(l + 1, 0)
            advance(l, 1)
            point(l + 2)
            if l == 0:
                spread(l + 1, 1)
            arrive(l + 1)
            prepare(l + 1)
            if l > 0:
                spread(l + 1, 1)
        else:
            finish(l, 0)
            finish(l, 1)

    for l in range(LAYERS):
        for s in range(SUBS):
            pltpu.make_async_remote_copy(
                cur[l][s].at[pl.ds(0, 2)], cur[l][s].at[pl.ds(0, 2)], hop_send.at[l, s], hop_recv.at[l, s],
                device_id=device(0, 0, 2, 0), device_id_type=MESH,
            ).wait_send()
            tiles = pl.ds(NEAR[1], 8 * 16 - NEAR[1])
            pltpu.make_async_remote_copy(
                stage.at[l, s, tiles], land[l][s].at[tiles], leaf_send.at[l, s], leaf_recv.at[l, s],
                device_id=device(0, 1, 0, 0), device_id_type=MESH,
            ).wait_send()
    for who in range(PIPE):
        n = {0: 4 + 1, 1: 4 + 1, 2: 6 + 1, 3: 6 + 1}[who]

        @functools.partial(at_y, who)
        def _():
            pltpu.make_async_remote_copy(
                wall.at[pl.ds(0, n)], wall.at[pl.ds(0, n)], w_send, w_recv.at[0, 0],
                device_id=device(1, 0, 0, 0), device_id_type=MESH,
            ).wait_send()


def on_device(features, weights, bias, layout):
    rs = 16 // SUBS
    n = bias.shape[1]
    return pl.pallas_call(
        kernel,
        name="sections",
        out_shape=jax.ShapeDtypeStruct(features.shape, jnp.bfloat16),
        in_specs=[
            pl.BlockSpec(memory_space=pltpu.VMEM),
            pl.BlockSpec(memory_space=pl.ANY),
            pl.BlockSpec(memory_space=pltpu.VMEM),
            pl.BlockSpec(memory_space=pltpu.VMEM),
        ],
        out_specs=pl.BlockSpec(memory_space=pltpu.VMEM),
        scratch_shapes=[
            pltpu.VMEM((LAYERS,) + weights.shape[1:], jnp.bfloat16),
            pltpu.VMEM((LAYERS, BD, 2 * K * BLOCK, 2 * BLOCK), jnp.bfloat16),
            pltpu.VMEM((PIPE, OWN, n), jnp.bfloat16),
            pltpu.VMEM((LAYERS, BD, 2 * BLOCK), jnp.float32),
            pltpu.VMEM((PIPE, OWN, ROWS // 2 + 8, 128), jnp.int32),
            pltpu.SMEM((PIPE, OWN, ROWS // 2 + 8, 128), jnp.int32),
            [[pltpu.VMEM((3, BD, rs, 128), jnp.bfloat16)] * SUBS] * LAYERS,
            pltpu.VMEM((LAYERS, SUBS, 128, rs, 128), jnp.bfloat16),
            [[pltpu.VMEM((128, rs, 128), jnp.bfloat16)] * SUBS] * LAYERS,
            pltpu.SemaphoreType.DMA((2,)),
            pltpu.SemaphoreType.DMA,
            pltpu.SemaphoreType.DMA,
            pltpu.SemaphoreType.DMA,
            pltpu.SemaphoreType.DMA,
            pltpu.SemaphoreType.DMA,
            pltpu.SemaphoreType.DMA((LAYERS, CHUNKS)),
            pltpu.SemaphoreType.DMA((LAYERS, SUBS)),
            pltpu.SemaphoreType.DMA((LAYERS, SUBS)),
            pltpu.SemaphoreType.DMA((LAYERS, SUBS)),
            pltpu.SemaphoreType.DMA((LAYERS, SUBS)),
        ],
        compiler_params=pltpu.CompilerParams(
            collective_id=0, has_side_effects=True, vmem_limit_bytes=60 * 1024 * 1024
        ),
    )(features, weights, bias, layout.reshape(OWN, ROWS // 2, 128))


def solution(mesh):
    in_specs = (
        P("pipe", "rows"),
        P("pipe", "rows", None, None),
        P("pipe", "rows"),
        P("pipe", None),
    )
    return jax.shard_map(
        on_device, mesh=mesh, in_specs=in_specs, out_specs=P("pipe", "rows"), check_vma=False
    )
```

```python
import functools

import jax
import jax.numpy as jnp
from jax import lax
from jax.experimental import pallas as pl
from jax.experimental.pallas import tpu as pltpu
from jax.sharding import PartitionSpec as P

MESH = pl.DeviceIdType.MESH
BLOCK = 64
K = 4
X, Z, C = 4, 8, 2
PIPE = 4
ROWS = X * Z * C
LAYERS = 8
OWN = LAYERS // PIPE
BD = 16
SUBS = 2
CHUNKS = 4
clamp_top = 32.0

OWN_PARTS = ((6, 1, (0,)), (10, -1, (0,)), (0, 0, (0,)))
RELAY_PARTS = ((8, 1, (1,)), (12, -1, (2,)), (2, 0, (1, 2)))
HERE = 6


def place():
    me = lax.axis_index("rows")
    return lax.axis_index("pipe"), me // (Z * C), (me // C) % Z, me % C


def device(dy, dx, dz, dc):
    y, x, z, c = place()
    row = (((x + dx + X) % X) * Z + (z + dz + Z) % Z) * C + (c + dc) % C
    return ((y + dy + PIPE) % PIPE, row)


def offsets():
    found = [(1, 0, 0, 0), (2, 0, 0, 0), (3, 0, 0, 0), (0, 0, 2, 0), (0, 0, -2, 0)]
    for dx in range(X):
        for dc in range(C):
            for dz in (0, 1, -1, 2 if dc == 0 else -2):
                here = (0, dx, dz, dc)
                if here not in found and here != (0, 0, 0, 0):
                    found.append(here)
    return found


def swap_halves(v):
    return pltpu.roll(v, BLOCK, 1)


def kernel(
    feat_ref, w_hbm, bias_ref, lay_ref, out_ref,
    wall, ready, biases, bias_tiles, tabs, stab, cur, near, stage, land,
    local_sem, smem_sem, tab_send, tab_recv, bias_send, bias_recv, w_send, w_recv,
    hop_send, hop_recv, leaf_send, leaf_recv,
):
    y, x, z, c = place()
    me = (x * Z + z) * C + c
    rs = cur[0][0].shape[1]
    left = lax.broadcasted_iota(jnp.int32, (BD, 128), 1) < BLOCK

    barrier = pltpu.get_barrier_semaphore()
    partners = offsets()
    for dy, dx, dz, dc in partners:
        pl.semaphore_signal(
            barrier, inc=1, device_id=device(-dy, -dx, -dz, -dc), device_id_type=MESH
        )

    own_w = pltpu.make_async_copy(w_hbm, wall.at[pl.ds(OWN * y, OWN)], local_sem.at[0])
    own_w.start()

    def fold(p, carry):
        cols = pl.ds(pl.multiple_of(p * 128, 128), 128)
        low = feat_ref[pl.ds(0, 16), cols].astype(jnp.float32)
        high = feat_ref[pl.ds(16, 16), cols].astype(jnp.float32)
        even = jnp.where(left, low, swap_halves(high)).astype(jnp.bfloat16)
        odd = jnp.where(left, swap_halves(low), high).astype(jnp.bfloat16)
        for s in range(SUBS):
            cur[0][s][2 * p] = even[s * rs : (s + 1) * rs]
            cur[0][s][2 * p + 1] = odd[s * rs : (s + 1) * rs]
        return carry

    lax.fori_loop(0, BD // 2, fold, 0)
    biases[pl.ds(y, 1)] = bias_ref[...].reshape(1, OWN, bias_ref.shape[1])

    lane = lax.broadcasted_iota(jnp.int32, (ROWS // 2, 128), 1)
    slot = lane & 63
    for a in range(OWN):
        entry = jnp.concatenate(
            [lay_ref[pl.ds(a, 1), pl.ds(i * 128, 128)] for i in range(ROWS // 2)], axis=0
        )
        owner = entry >> 4
        key = slot * BD + (entry & 15)
        table = jnp.zeros((ROWS // 2, 128), jnp.int32)
        for q, dz in enumerate((0, -2, 2)):
            source = (x * Z + (z + dz + Z) % Z) * C + c
            for half in range(2):
                hit = (owner == source) & ((lane >> 6) == half)
                first = jnp.min(jnp.where(hit, key, 1 << 20), axis=1, keepdims=True) & 15
                last = jnp.max(jnp.where(hit, key, 0), axis=1, keepdims=True) & 15
                table = jnp.where(lane == 4 * q + 2 * half, first, table)
                table = jnp.where(lane == 4 * q + 2 * half + 1, last, table)
        tabs[y, a, pl.ds(0, ROWS // 2)] = table
    mine = jnp.concatenate(
        [lay_ref[:, pl.ds(pl.multiple_of((x * Z + z) * 128, 128), 128)]]
        + [jnp.zeros((8 - OWN, 128), jnp.int32)],
        axis=0,
    )
    owner = mine >> 4
    spot = lax.broadcasted_iota(jnp.int32, (8, 128), 1) & 63
    rank = jnp.zeros((8, 128), jnp.int32)
    for step in range(1, 64):
        same = (pltpu.roll(owner, step, 1) == owner) & (spot >= step)
        rank = jnp.where(same, 1, rank)
    dx = (x - (owner >> 4) + X) & (X - 1)
    dz = (z - ((owner >> 1) & (Z - 1)) + Z) & (Z - 1)
    dc = (c + owner) & 1
    base = jnp.zeros((8, 128), jnp.int32)
    for d, at in ((0, 0), (2, 2), (6, 4), (1, 6), (3, 8), (7, 10), (5, 12), (4, 14)):
        base = jnp.where(dz == d, at, base)
    where = (dx * 2 + dc) * 16 + base + rank
    for a in range(OWN):
        tabs[y, a, pl.ds(ROWS // 2, 8)] = jnp.broadcast_to(where[a : a + 1], (8, 128))

    with jax.named_scope("barrier_wait"):
        pl.semaphore_wait(barrier, len(partners))

    def tab_copy(dy):
        return pltpu.make_async_remote_copy(
            tabs.at[y], tabs.at[y], tab_send, tab_recv.at[y],
            device_id=device(dy, 0, 0, 0), device_id_type=MESH,
        )

    def bias_copy(dy):
        return pltpu.make_async_remote_copy(
            biases.at[y], biases.at[y], bias_send, bias_recv,
            device_id=device(dy, 0, 0, 0), device_id_type=MESH,
        )

    def hop(l, s, dz, q):
        return pltpu.make_async_remote_copy(
            cur[l][s], near[l][s].at[q], hop_send.at[l, s], hop_recv.at[l, s],
            device_id=device(0, 0, dz, 0), device_id_type=MESH,
        )

    def start_hops(l, s):
        hop(l, s, 2, 0).start()
        hop(l, s, -2, 1).start()

    rows = BD // CHUNKS

    def w_copy(l, chunk, dy, src):
        piece = pl.ds(chunk * rows, rows)
        return pltpu.make_async_remote_copy(
            src.at[piece], wall.at[l, piece], w_send, w_recv.at[l, chunk],
            device_id=device(dy, 0, 0, 0), device_id_type=MESH,
        )

    def w_own(a, dy, order):
        for chunk in order:
            w_copy(OWN * y + a, chunk, dy, w_hbm.at[a]).start()

    def w_wait(l, order):
        for chunk in order:
            w_copy(l, chunk, 1, wall.at[l]).wait_recv()

    def w_pass(l, order, dy):
        for chunk in order:
            w_wait(l, (chunk,))
            w_copy(l, chunk, dy, wall.at[l]).start()

    def at_y(which, act):
        pl.when(y == which)(act)

    first_half, last_half, forward, turned = (0, 1), (2, 3), (0, 1, 2, 3), (2, 3, 0, 1)

    both, ahead, behind = (1, -1), (1,), (-1,)
    program = (
        (
            (0, ("own", 0, both, forward), ("own", 1, both, forward)),
            (1, ("own", 0, behind, turned), ("own", 1, behind, turned)),
            (2, ("own", 0, both, forward), ("own", 1, both, forward)),
            (3, ("own", 0, ahead, forward), ("own", 1, ahead, forward)),
        ),
        (
            (1, ("pass", 0, ahead, first_half), ("own", 0, ahead, forward), ("own", 1, ahead, forward)),
            (3, ("pass", 0, behind, last_half)),
        ),
        (
            (0, ("pass", 2, behind, last_half), ("pass", 3, behind, last_half)),
            (2, ("pass", 2, ahead, first_half)),
            (3, ("pass", 1, behind, forward), ("own", 0, behind, turned), ("own", 1, behind, turned)),
        ),
        (
            (0, ("pass", 6, ahead, first_half), ("pass", 7, ahead, first_half)),
            (1, ("pass", 4, behind, last_half), ("pass", 5, behind, last_half)),
            (2, ("pass", 3, ahead, first_half)),
            (3, ("pass", 4, ahead, first_half), ("pass", 5, ahead, first_half)),
        ),
        (
            (2, ("pass", 6, behind, last_half), ("pass", 7, behind, last_half)),
        ),
    )

    def point(p):
        for who, *acts in program[p] if p < len(program) else ():
            @functools.partial(at_y, who)
            def _():
                for kind, which, ways, order in acts:
                    for dy in ways:
                        if kind == "own":
                            w_own(which, dy, order)
                        else:
                            w_pass(which, order, dy)

    def arrive(l):
        own = l // OWN
        for who in range(PIPE):
            passed = [
                chunk
                for step in program for y_at, *acts in step if y_at == who
                for kind, which, _, order in acts if kind == "pass" and which == l
                for chunk in order
            ]
            order = tuple(chunk for chunk in forward if chunk not in passed)
            if who != own and order:
                at_y(who, functools.partial(w_wait, l, order))
        if l % OWN == 0:
            at_y(own, own_w.wait)

    def prepare(l):
        keep = lax.broadcasted_iota(jnp.int32, (BLOCK, 128), 1) < BLOCK

        def one(r, carry):
            for p in range(2):
                raw = wall[l, r, :, pl.ds(p * 128, 128)].astype(jnp.float32)
                turn = swap_halves(raw)
                zero = jnp.zeros_like(raw)
                parts = (
                    jnp.where(keep, raw, zero), jnp.where(keep, zero, turn),
                    jnp.where(keep, turn, zero), jnp.where(keep, zero, raw),
                )
                for i, part in enumerate(parts):
                    ready[l, r, pl.ds((p * 4 + i) * BLOCK, BLOCK), :] = part.astype(jnp.bfloat16)
            return carry

        lax.fori_loop(0, BD, one, 0, unroll=4)

        line_left = lax.broadcasted_iota(jnp.int32, (1, 128), 1) < BLOCK

        for p in range(BD // 2):
            row = biases[l // OWN, pl.ds(l % OWN, 1), pl.ds(p * 128, 128)].astype(jnp.float32)
            turn = swap_halves(row)
            bias_tiles[l, pl.ds(2 * p, 1), :] = jnp.where(line_left, row, turn)
            bias_tiles[l, pl.ds(2 * p + 1, 1), :] = jnp.where(line_left, turn, row)

    def leaf(l, s, u, dx, dz, dc, at, n):
        tiles = pl.ds(u * 16 + at, n)
        return pltpu.make_async_remote_copy(
            stage.at[l, s, tiles], land[l][s].at[tiles], leaf_send.at[l, s], leaf_recv.at[l, s],
            device_id=device(0, dx, dz, dc), device_id_type=MESH,
        )

    def hop_wait(l, s):
        pltpu.make_async_remote_copy(
            near[l][s], near[l][s], hop_send.at[l, s], hop_recv.at[l, s],
            device_id=device(0, 0, 2, 0), device_id_type=MESH,
        ).wait_recv()

    def columns(l, s, parts, far):
        def column(t, carry):
            dx = (t // 2) ^ 2
            dc = t % 2
            u = dx * 2 + dc
            cc = (c + dc) % C
            xx = ((x + dx) % X) * Z
            todo = parts
            if far:
                todo = ((14, 2 - 4 * dc, (1 + dc,)),) + parts
            moves = []
            for at, dz, sources in todo:
                for i, q in enumerate(sources):
                    for k in range(2):
                        index = stab[l // OWN, l % OWN, xx + (z + dz + Z) % Z, 4 * q + 2 * cc + k]
                        moves.append((u * 16 + at + 2 * i + k, q, index))
            tiles = [near[l][s][q - 1, i] if far else cur[l][s][i] for _, q, i in moves]
            for (at, _, _), tile in zip(moves, tiles):
                stage[l, s, at] = tile
            for at, dz, sources in todo:
                go = leaf(l, s, u, dx, dz, dc, at, 2 * len(sources))
                if isinstance(dz, int) and dz == 0:
                    pl.when(u > 0)(go.start)
                else:
                    go.start()
            return carry

        lax.fori_loop(0, X * C, column, 0)
        for at, dz, sources in parts:
            if dz == 0:
                for k in range(at, at + 2 * len(sources)):
                    land[l][s][k] = stage[l, s, k]

    def pack_own(l, s):
        columns(l, s, OWN_PARTS, False)

    def pack(l, s):
        columns(l, s, RELAY_PARTS, True)

    def spread(l, s):
        hop_wait(l, s)
        pack(l, s)

    def gather(l, s):
        tiles = pl.ds(HERE, 8 * 16 - HERE)
        pltpu.make_async_remote_copy(
            stage.at[l, s, tiles], land[l][s].at[tiles], leaf_send.at[l, s], leaf_recv.at[l, s],
            device_id=device(0, 1, 0, 0), device_id_type=MESH,
        ).wait_recv()

    def block_out(l, s, r):
        row = stab.at[l // OWN, l % OWN, ROWS // 2]
        lhs = jnp.concatenate([land[l][s][row[c * 64 + r * K + k]] for k in range(K)], axis=1)
        total = jnp.dot(lhs, ready[l, r], preferred_element_type=jnp.float32)
        total = total + bias_tiles[l, pl.ds(r, 1), :]
        return jnp.minimum(jnp.maximum(total, 0.0), clamp_top)

    def advance(l, s):
        gather(l, s)
        compute(l, s)
        start_hops(l + 1, s)
        pack_own(l + 1, s)

    def compute(l, s):
        def pair(p, carry):
            for r in range(2):
                cur[l + 1][s][2 * p + r] = block_out(l, s, 2 * p + r).astype(jnp.bfloat16)
            return carry

        lax.fori_loop(0, BD // 2, pair, 0, unroll=8)

    def finish(l, s):
        gather(l, s)
        finish_compute(l, s)

    def finish_compute(l, s):
        half = left[:rs]

        def pair(p, carry):
            even, odd = block_out(l, s, 2 * p), block_out(l, s, 2 * p + 1)
            cols = pl.ds(pl.multiple_of(p * 128, 128), 128)
            low = jnp.where(half, even, swap_halves(odd))
            high = jnp.where(half, swap_halves(even), odd)
            out_ref[pl.ds(s * rs, rs), cols] = low.astype(jnp.bfloat16)
            out_ref[pl.ds(16 + s * rs, rs), cols] = high.astype(jnp.bfloat16)
            return carry

        lax.fori_loop(0, BD // 2, pair, 0, unroll=8)

    def tab_wait(who):
        @pl.when(y != who)
        def _():
            pltpu.make_async_remote_copy(
                tabs.at[who], tabs.at[who], tab_send, tab_recv.at[who],
                device_id=device(1, 0, 0, 0), device_id_type=MESH,
            ).wait_recv()

    def to_smem(l):
        at = (l // OWN, l % OWN)
        return pltpu.make_async_copy(tabs.at[at], stab.at[at], smem_sem.at[l])

    def smem_wait(l):
        to_smem(l).wait()

    for dy in (2, 1, 3):
        tab_copy(dy).start()
    for s in range(SUBS):
        start_hops(0, s)
    for dy in (1, 2, 3):
        bias_copy(dy).start()
    point(0)
    tab_wait(0)
    to_smem(0).start()
    to_smem(1).start()
    smem_wait(0)
    for s in range(SUBS):
        pack_own(0, s)
    for s in range(SUBS):
        spread(0, s)
    for who in range(1, PIPE):
        tab_wait(who)
        for a in range(OWN):
            to_smem(who * OWN + a).start()
    pltpu.make_async_remote_copy(
        biases.at[pl.ds(0, 3)], biases.at[pl.ds(0, 3)], bias_send, bias_recv,
        device_id=device(1, 0, 0, 0), device_id_type=MESH,
    ).wait()
    point(1)
    arrive(0)
    prepare(0)
    last = LAYERS - 1
    order = [(l, s) for l in range(LAYERS) for s in range(SUBS)]
    lag = 1 if SUBS > 2 else 0
    for n, (l, s) in enumerate(order):
        if s == 0 and l < last:
            smem_wait(l + 1)
        if l < last:
            advance(l, s)
        else:
            finish(l, s)
        late = l == 0
        if s == SUBS - 1 and l < last:
            point(l + 2)
            if not late:
                arrive(l + 1)
                prepare(l + 1)
        if n >= lag:
            behind_l, behind_s = order[n - lag]
            if behind_l < last:
                spread(behind_l + 1, behind_s)
        if s == SUBS - 1 and late:
            arrive(l + 1)
            prepare(l + 1)

    pltpu.make_async_remote_copy(
        tabs.at[pl.ds(0, 3)], tabs.at[pl.ds(0, 3)], tab_send, tab_recv.at[0],
        device_id=device(1, 0, 0, 0), device_id_type=MESH,
    ).wait_send()
    for l in range(LAYERS):
        for s in range(SUBS):
            pltpu.make_async_remote_copy(
                near[l][s], near[l][s], hop_send.at[l, s], hop_recv.at[l, s],
                device_id=device(0, 0, 2, 0), device_id_type=MESH,
            ).wait_send()
            tiles = pl.ds(HERE, 8 * 16 - HERE)
            pltpu.make_async_remote_copy(
                stage.at[l, s, tiles], land[l][s].at[tiles], leaf_send.at[l, s], leaf_recv.at[l, s],
                device_id=device(0, 1, 0, 0), device_id_type=MESH,
            ).wait_send()
    for who in range(PIPE):
        pieces = sum(
            len(order) * len(ways)
            for step in program for y_at, *acts in step if y_at == who
            for _, _, ways, order in acts
        )

        @functools.partial(at_y, who)
        def _():
            pltpu.make_async_remote_copy(
                wall.at[:, pl.ds(0, pieces * rows // LAYERS)],
                wall.at[:, pl.ds(0, pieces * rows // LAYERS)],
                w_send, w_recv.at[0, 0],
                device_id=device(1, 0, 0, 0), device_id_type=MESH,
            ).wait_send()


def on_device(features, weights, bias, layout):
    rs = 16 // SUBS
    n = bias.shape[1]
    return pl.pallas_call(
        kernel,
        name="sections",
        out_shape=jax.ShapeDtypeStruct(features.shape, jnp.bfloat16),
        in_specs=[
            pl.BlockSpec(memory_space=pltpu.VMEM),
            pl.BlockSpec(memory_space=pl.ANY),
            pl.BlockSpec(memory_space=pltpu.VMEM),
            pl.BlockSpec(memory_space=pltpu.VMEM),
        ],
        out_specs=pl.BlockSpec(memory_space=pltpu.VMEM),
        scratch_shapes=[
            pltpu.VMEM((LAYERS,) + weights.shape[1:], jnp.bfloat16),
            pltpu.VMEM((LAYERS, BD, 2 * K * BLOCK, 2 * BLOCK), jnp.bfloat16),
            pltpu.VMEM((PIPE, OWN, n), jnp.bfloat16),
            pltpu.VMEM((LAYERS, BD, 2 * BLOCK), jnp.float32),
            pltpu.VMEM((PIPE, OWN, ROWS // 2 + 8, 128), jnp.int32),
            pltpu.SMEM((PIPE, OWN, ROWS // 2 + 8, 128), jnp.int32),
            [[pltpu.VMEM((BD, rs, 128), jnp.bfloat16)] * SUBS] * LAYERS,
            [[pltpu.VMEM((2, BD, rs, 128), jnp.bfloat16)] * SUBS] * LAYERS,
            pltpu.VMEM((LAYERS, SUBS, 128, rs, 128), jnp.bfloat16),
            [[pltpu.VMEM((128, rs, 128), jnp.bfloat16)] * SUBS] * LAYERS,
            pltpu.SemaphoreType.DMA((1,)),
            pltpu.SemaphoreType.DMA((LAYERS,)),
            pltpu.SemaphoreType.DMA,
            pltpu.SemaphoreType.DMA((PIPE,)),
            pltpu.SemaphoreType.DMA,
            pltpu.SemaphoreType.DMA,
            pltpu.SemaphoreType.DMA,
            pltpu.SemaphoreType.DMA((LAYERS, CHUNKS)),
            pltpu.SemaphoreType.DMA((LAYERS, SUBS)),
            pltpu.SemaphoreType.DMA((LAYERS, SUBS)),
            pltpu.SemaphoreType.DMA((LAYERS, SUBS)),
            pltpu.SemaphoreType.DMA((LAYERS, SUBS)),
        ],
        compiler_params=pltpu.CompilerParams(
            collective_id=0, has_side_effects=True, vmem_limit_bytes=60 * 1024 * 1024
        ),
    )(features, weights, bias, layout)


def solution(mesh):
    in_specs = (
        P("pipe", "rows"),
        P("pipe", "rows", None, None),
        P("pipe", "rows"),
        P("pipe", None),
    )
    return jax.shard_map(
        on_device, mesh=mesh, in_specs=in_specs, out_specs=P("pipe", "rows"), check_vma=False
    )
```

```python
import functools

import jax
import jax.numpy as jnp
from jax import lax
from jax.experimental import pallas as pl
from jax.experimental.pallas import tpu as pltpu
from jax.sharding import PartitionSpec as P

MESH = pl.DeviceIdType.MESH
BLOCK = 64
K = 4
X, Z, C = 4, 8, 2
PIPE = 4
ROWS = X * Z * C
LAYERS = 8
OWN = LAYERS // PIPE
BD = 16
SUBS = 4
LAG = 1
CHUNKS = 4
clamp_top = 32.0

OWN_PARTS = ((6, 1, (0,)), (10, -1, (0,)), (0, 0, (0,)))
RELAY_PARTS = ((8, 1, (1,)), (12, -1, (2,)), (2, 0, (1, 2)))
HERE = 6


def place():
    me = lax.axis_index("rows")
    return lax.axis_index("pipe"), me >> 4, (me >> 1) & (Z - 1), me & (C - 1)


def device(dy, dx, dz, dc):
    y, x, z, c = place()
    row = (((x + dx) & (X - 1)) << 4) | (((z + dz) & (Z - 1)) << 1) | ((c ^ dc) & (C - 1))
    return ((y + dy) & (PIPE - 1), row)


def offsets():
    found = [(1, 0, 0, 0), (2, 0, 0, 0), (3, 0, 0, 0), (0, 0, 2, 0), (0, 0, -2, 0)]
    for dx in range(X):
        for dc in range(C):
            for dz in (0, 1, -1, 2 if dc == 0 else -2):
                here = (0, dx, dz, dc)
                if here not in found and here != (0, 0, 0, 0):
                    found.append(here)
    return found


def swap_halves(v):
    return pltpu.roll(v, BLOCK, 1)


def kernel(
    feat_ref, w_hbm, bias_ref, lay_ref, out_ref,
    wall, ready, biases, bias_tiles, tabs, stab, cur, near, stage, land,
    local_sem, smem_sem, tab_send, tab_recv, bias_send, bias_recv, w_send, w_recv,
    hop_send, hop_recv, leaf_send, leaf_recv,
):
    y, x, z, c = place()
    me = (x * Z + z) * C + c
    rs = cur[0][0].shape[1]
    left = lax.broadcasted_iota(jnp.int32, (BD, 128), 1) < BLOCK

    barrier = pltpu.get_barrier_semaphore()
    partners = offsets()
    for dy, dx, dz, dc in partners:
        pl.semaphore_signal(
            barrier, inc=1, device_id=device(-dy, -dx, -dz, -dc), device_id_type=MESH
        )

    own_w = pltpu.make_async_copy(w_hbm, wall.at[pl.ds(OWN * y, OWN)], local_sem.at[0])
    own_w.start()

    def fold(p, carry):
        cols = pl.ds(pl.multiple_of(p * 128, 128), 128)
        low = feat_ref[pl.ds(0, 16), cols].astype(jnp.float32)
        high = feat_ref[pl.ds(16, 16), cols].astype(jnp.float32)
        even = jnp.where(left, low, swap_halves(high)).astype(jnp.bfloat16)
        odd = jnp.where(left, swap_halves(low), high).astype(jnp.bfloat16)
        for s in range(SUBS):
            cur[0][s][2 * p] = even[s * rs : (s + 1) * rs]
            cur[0][s][2 * p + 1] = odd[s * rs : (s + 1) * rs]
        return carry

    lax.fori_loop(0, BD // 2, fold, 0)
    biases[pl.ds(y, 1)] = bias_ref[...].reshape(1, OWN, bias_ref.shape[1])

    lane = lax.broadcasted_iota(jnp.int32, (ROWS // 2, 128), 1)
    slot = lane & 63
    for a in range(OWN):
        entry = jnp.concatenate(
            [lay_ref[pl.ds(a, 1), pl.ds(i * 128, 128)] for i in range(ROWS // 2)], axis=0
        )
        owner = entry >> 4
        key = slot * BD + (entry & 15)
        for half in range(2):
            table = jnp.zeros((ROWS // 2, 128), jnp.int32)
            for q, dz in enumerate((0, -2, 2)):
                source = (x << 4) | (((z + dz) & (Z - 1)) << 1) | c
                hit = (owner == source) & ((lane >> 6) == half)
                first = jnp.min(jnp.where(hit, key, 1 << 20), axis=1, keepdims=True) & 15
                last = jnp.max(jnp.where(hit, key, 0), axis=1, keepdims=True) & 15
                table = jnp.where(lane == 2 * q, first, table)
                table = jnp.where(lane == 2 * q + 1, last, table)
            tabs[y, a, pl.ds(half * ROWS // 2, ROWS // 2)] = table
    mine = jnp.concatenate(
        [lay_ref[:, pl.ds(pl.multiple_of((x * Z + z) * 128, 128), 128)]]
        + [jnp.zeros((8 - OWN, 128), jnp.int32)],
        axis=0,
    )
    owner = mine >> 4
    spot = lax.broadcasted_iota(jnp.int32, (8, 128), 1) & 63
    rank = jnp.zeros((8, 128), jnp.int32)
    for step in range(1, 64):
        same = (pltpu.roll(owner, step, 1) == owner) & (spot >= step)
        rank = jnp.where(same, 1, rank)
    dx = (x - (owner >> 4) + X) & (X - 1)
    dz = (z - ((owner >> 1) & (Z - 1)) + Z) & (Z - 1)
    dc = (c + owner) & 1
    base = jnp.zeros((8, 128), jnp.int32)
    for d, at in ((0, 0), (2, 2), (6, 4), (1, 6), (3, 8), (7, 10), (5, 12), (4, 14)):
        base = jnp.where(dz == d, at, base)
    where = (dx * 2 + dc) * 16 + base + rank
    for a in range(OWN):
        both_rows = jnp.concatenate(
            [where[a : a + 1], pltpu.roll(where, 64, 1)[a : a + 1], jnp.zeros((6, 128), jnp.int32)], axis=0
        )
        tabs[y, a, pl.ds(ROWS, 8)] = both_rows

    with jax.named_scope("barrier_wait"):
        pl.semaphore_wait(barrier, len(partners))

    def tab_copy(dy):
        return pltpu.make_async_remote_copy(
            tabs.at[y], tabs.at[y], tab_send, tab_recv.at[y],
            device_id=device(dy, 0, 0, 0), device_id_type=MESH,
        )

    def bias_copy(dy):
        return pltpu.make_async_remote_copy(
            biases.at[y], biases.at[y], bias_send, bias_recv,
            device_id=device(dy, 0, 0, 0), device_id_type=MESH,
        )

    def hop(l, s, dz, q):
        return pltpu.make_async_remote_copy(
            cur[l][s], near[l][s].at[q], hop_send.at[l, s], hop_recv.at[l, s],
            device_id=device(0, 0, dz, 0), device_id_type=MESH,
        )

    def start_hops(l, s):
        hop(l, s, 2, 0).start()
        hop(l, s, -2, 1).start()

    rows = BD // CHUNKS

    def w_copy(l, chunk, dy, src):
        piece = pl.ds(chunk * rows, rows)
        return pltpu.make_async_remote_copy(
            src.at[piece], wall.at[l, piece], w_send, w_recv.at[l, chunk],
            device_id=device(dy, 0, 0, 0), device_id_type=MESH,
        )

    def w_own(a, dy, order):
        for chunk in order:
            w_copy(OWN * y + a, chunk, dy, w_hbm.at[a]).start()

    def w_wait(l, order):
        for chunk in order:
            w_copy(l, chunk, 1, wall.at[l]).wait_recv()

    def w_pass(l, order, dy):
        for chunk in order:
            w_wait(l, (chunk,))
            w_copy(l, chunk, dy, wall.at[l]).start()

    def at_y(which, act):
        pl.when(y == which)(act)


    h1, h2 = (0, 1), (2, 3)

    def own(which, *ways):
        return tuple(
            ("own", which, dy, chunks or (h1 + h2 if dy > 0 else h2 + h1)) for dy, chunks in ways
        )

    def fwd(l, dy, chunks):
        return (("pass", l, dy, chunks),)

    up, down = (1, None), (-1, None)
    program = {
        "start": (
            (0, own(0, up, down)),
            (1, own(0, down) + own(1, down)),
            (2, own(0, up, down) + own(1, up, down)),
            (3, own(0, up) + own(1, up)),
        ),
        "first": ((0, own(1, up, down)), (1, fwd(0, 1, h1)), (3, fwd(0, -1, h2))),
        (0, 1): ((1, fwd(1, 1, (0,))), (3, fwd(1, -1, (2,)))),
        (0, 2): ((1, fwd(1, 1, (1,)) + own(0, (1, h1))), (3, fwd(1, -1, (3,)))),
        (0, 3): ((0, fwd(2, -1, h2) + fwd(3, -1, h2)),),
        (1, 0): ((1, own(1, (1, h1))),),
        (1, 1): ((2, fwd(2, 1, (0,))), (3, fwd(2, -1, (2,)))),
        (1, 3): ((2, fwd(2, 1, (1,))), (3, fwd(2, -1, (3,)))),
        (2, 0): ((2, fwd(3, 1, h1)),),
        (2, 1): (
            (0, fwd(6, 1, h1) + fwd(7, 1, h1)),
            (1, fwd(4, -1, h2) + fwd(5, -1, h2)),
            (3, fwd(3, -1, h2) + fwd(4, 1, h1) + fwd(5, 1, h1)),
        ),
        (2, 3): ((3, own(0, down) + own(1, down)),),
        (4, 0): ((2, fwd(6, -1, h2)),),
        (5, 0): ((2, fwd(7, -1, h2)),),
    }

    def acts_of(who):
        return [act for step in program.values() for y_at, acts in step if y_at == who for act in acts]

    def point(*at):
        for who, acts in program.get(at if len(at) > 1 else at[0], ()):
            @functools.partial(at_y, who)
            def _():
                for kind, which, dy, order in acts:
                    if kind == "own":
                        w_own(which, dy, order)
                    else:
                        w_pass(which, order, dy)

    def arrive(l):
        owner = l // OWN
        for who in range(PIPE):
            passed = [
                chunk
                for kind, which, _, order in acts_of(who) if kind == "pass" and which == l
                for chunk in order
            ]
            order = tuple(chunk for chunk in h1 + h2 if chunk not in passed)
            if who != owner and order:
                at_y(who, functools.partial(w_wait, l, order))
        if l % OWN == 0:
            at_y(owner, own_w.wait)

    def prepare(l):
        keep = lax.broadcasted_iota(jnp.int32, (BLOCK, 128), 1) < BLOCK

        def one(r, carry):
            for p in range(2):
                raw = wall[l, r, :, pl.ds(p * 128, 128)].astype(jnp.float32)
                turn = swap_halves(raw)
                zero = jnp.zeros_like(raw)
                parts = (
                    jnp.where(keep, raw, zero), jnp.where(keep, zero, turn),
                    jnp.where(keep, turn, zero), jnp.where(keep, zero, raw),
                )
                for i, part in enumerate(parts):
                    ready[l, r, pl.ds((p * 4 + i) * BLOCK, BLOCK), :] = part.astype(jnp.bfloat16)
            return carry

        lax.fori_loop(0, BD, one, 0, unroll=4)

        line_left = lax.broadcasted_iota(jnp.int32, (1, 128), 1) < BLOCK

        for p in range(BD // 2):
            row = biases[l // OWN, pl.ds(l % OWN, 1), pl.ds(p * 128, 128)].astype(jnp.float32)
            turn = swap_halves(row)
            bias_tiles[l, pl.ds(2 * p, 1), :] = jnp.where(line_left, row, turn)
            bias_tiles[l, pl.ds(2 * p + 1, 1), :] = jnp.where(line_left, turn, row)

    def leaf(l, s, base, dx, dz, dc, at, n):
        tiles = pl.ds(base + at, n)
        return pltpu.make_async_remote_copy(
            stage.at[l, s, tiles], land[l][s].at[tiles], leaf_send.at[l, s], leaf_recv.at[l, s],
            device_id=device(0, dx, dz, dc), device_id_type=MESH,
        )

    def hop_wait(l, s):
        pltpu.make_async_remote_copy(
            near[l][s], near[l][s], hop_send.at[l, s], hop_recv.at[l, s],
            device_id=device(0, 0, 2, 0), device_id_type=MESH,
        ).wait_recv()

    def columns(l, s, parts, far):
        def column(t, carry):
            dx = t ^ 2
            xx = ((x + dx) & (X - 1)) << 3
            plans = []
            for dc in range(C):
                todo = parts
                if far:
                    todo = ((14, 2 - 4 * dc, (1 + dc,)),) + parts
                plans.append((dc, (dx * 2 + dc) * 16, todo))
            moves = []
            for dc, base, todo in plans:
                for at, dz, sources in todo:
                    row = ((c ^ dc) << 5) | xx | ((z + dz) & (Z - 1))
                    for i, q in enumerate(sources):
                        for k in range(2):
                            index = stab[l // OWN, l % OWN, row, 2 * q + k]
                            moves.append((base + at + 2 * i + k, q, index))
            tiles = [near[l][s][q - 1, i] if far else cur[l][s][i] for _, q, i in moves]
            for (at, _, _), tile in zip(moves, tiles):
                stage[l, s, at] = tile
            for dc, base, todo in plans:
                for at, dz, sources in todo:
                    go = leaf(l, s, base, dx, dz, dc, at, 2 * len(sources))
                    if dz == 0 and dc == 0:
                        pl.when(dx > 0)(go.start)
                    else:
                        go.start()
            return carry

        lax.fori_loop(0, X, column, 0)
        for at, dz, sources in parts:
            if dz == 0:
                for k in range(at, at + 2 * len(sources)):
                    land[l][s][k] = stage[l, s, k]

    def pack_own(l, s):
        columns(l, s, OWN_PARTS, False)

    def pack(l, s):
        columns(l, s, RELAY_PARTS, True)

    def spread(l, s):
        hop_wait(l, s)
        pack(l, s)

    def gather(l, s):
        tiles = pl.ds(HERE, 8 * 16 - HERE)
        pltpu.make_async_remote_copy(
            stage.at[l, s, tiles], land[l][s].at[tiles], leaf_send.at[l, s], leaf_recv.at[l, s],
            device_id=device(0, 1, 0, 0), device_id_type=MESH,
        ).wait_recv()

    def block_out(l, s, r):
        row = stab.at[l // OWN, l % OWN, ROWS + c]
        lhs = jnp.concatenate([land[l][s][row[r * K + k]] for k in range(K)], axis=1)
        total = jnp.dot(lhs, ready[l, r], preferred_element_type=jnp.float32)
        total = total + bias_tiles[l, pl.ds(r, 1), :]
        return jnp.minimum(jnp.maximum(total, 0.0), clamp_top)

    def advance(l, s):
        gather(l, s)
        compute(l, s)
        start_hops(l + 1, s)
        pack_own(l + 1, s)

    def compute(l, s):
        def pair(p, carry):
            for r in range(2):
                cur[l + 1][s][2 * p + r] = block_out(l, s, 2 * p + r).astype(jnp.bfloat16)
            return carry

        lax.fori_loop(0, BD // 2, pair, 0, unroll=8)

    def finish(l, s):
        gather(l, s)
        finish_compute(l, s)

    def finish_compute(l, s):
        half = left[:rs]

        def pair(p, carry):
            even, odd = block_out(l, s, 2 * p), block_out(l, s, 2 * p + 1)
            cols = pl.ds(pl.multiple_of(p * 128, 128), 128)
            low = jnp.where(half, even, swap_halves(odd))
            high = jnp.where(half, swap_halves(even), odd)
            out_ref[pl.ds(s * rs, rs), cols] = low.astype(jnp.bfloat16)
            out_ref[pl.ds(16 + s * rs, rs), cols] = high.astype(jnp.bfloat16)
            return carry

        lax.fori_loop(0, BD // 2, pair, 0, unroll=8)

    def tab_wait(who):
        @pl.when(y != who)
        def _():
            pltpu.make_async_remote_copy(
                tabs.at[who], tabs.at[who], tab_send, tab_recv.at[who],
                device_id=device(1, 0, 0, 0), device_id_type=MESH,
            ).wait_recv()

    def to_smem(l):
        at = (l // OWN, l % OWN)
        return pltpu.make_async_copy(tabs.at[at], stab.at[at], smem_sem.at[l])

    def smem_wait(l):
        to_smem(l).wait()

    for dy in (2, 1, 3):
        tab_copy(dy).start()
    for s in range(SUBS):
        start_hops(0, s)
    for dy in (1, 2, 3):
        bias_copy(dy).start()
    point("start")
    tab_wait(0)
    to_smem(0).start()
    to_smem(1).start()
    smem_wait(0)
    for s in range(SUBS):
        pack_own(0, s)
    for s in range(SUBS):
        spread(0, s)
    for who in range(1, PIPE):
        tab_wait(who)
        for a in range(OWN):
            to_smem(who * OWN + a).start()
    pltpu.make_async_remote_copy(
        biases.at[pl.ds(0, 3)], biases.at[pl.ds(0, 3)], bias_send, bias_recv,
        device_id=device(1, 0, 0, 0), device_id_type=MESH,
    ).wait()
    point("first")
    arrive(0)
    prepare(0)
    last = LAYERS - 1
    order = [(l, s) for l in range(LAYERS) for s in range(SUBS)]
    for n, (l, s) in enumerate(order):
        if s == 0 and l < last:
            smem_wait(l + 1)
        if l < last:
            advance(l, s)
        else:
            finish(l, s)
        point(l, s)
        if s == SUBS - 1 and 0 < l < last:
            arrive(l + 1)
            prepare(l + 1)
        if n >= LAG:
            behind_l, behind_s = order[n - LAG]
            if behind_l < last:
                spread(behind_l + 1, behind_s)
        if s == SUBS - 1 and l == 0:
            arrive(l + 1)
            prepare(l + 1)

    pltpu.make_async_remote_copy(
        tabs.at[pl.ds(0, 3)], tabs.at[pl.ds(0, 3)], tab_send, tab_recv.at[0],
        device_id=device(1, 0, 0, 0), device_id_type=MESH,
    ).wait_send()
    for l in range(LAYERS):
        for s in range(SUBS):
            pltpu.make_async_remote_copy(
                near[l][s], near[l][s], hop_send.at[l, s], hop_recv.at[l, s],
                device_id=device(0, 0, 2, 0), device_id_type=MESH,
            ).wait_send()
            tiles = pl.ds(HERE, 8 * 16 - HERE)
            pltpu.make_async_remote_copy(
                stage.at[l, s, tiles], land[l][s].at[tiles], leaf_send.at[l, s], leaf_recv.at[l, s],
                device_id=device(0, 1, 0, 0), device_id_type=MESH,
            ).wait_send()
    for who in range(PIPE):
        pieces = sum(len(order) for _, _, _, order in acts_of(who))

        @functools.partial(at_y, who)
        def _():
            pltpu.make_async_remote_copy(
                wall.at[:, pl.ds(0, pieces * rows // LAYERS)],
                wall.at[:, pl.ds(0, pieces * rows // LAYERS)],
                w_send, w_recv.at[0, 0],
                device_id=device(1, 0, 0, 0), device_id_type=MESH,
            ).wait_send()


def on_device(features, weights, bias, layout):
    rs = 16 // SUBS
    n = bias.shape[1]
    return pl.pallas_call(
        kernel,
        name="sections",
        out_shape=jax.ShapeDtypeStruct(features.shape, jnp.bfloat16),
        in_specs=[
            pl.BlockSpec(memory_space=pltpu.VMEM),
            pl.BlockSpec(memory_space=pl.ANY),
            pl.BlockSpec(memory_space=pltpu.VMEM),
            pl.BlockSpec(memory_space=pltpu.VMEM),
        ],
        out_specs=pl.BlockSpec(memory_space=pltpu.VMEM),
        scratch_shapes=[
            pltpu.VMEM((LAYERS,) + weights.shape[1:], jnp.bfloat16),
            pltpu.VMEM((LAYERS, BD, 2 * K * BLOCK, 2 * BLOCK), jnp.bfloat16),
            pltpu.VMEM((PIPE, OWN, n), jnp.bfloat16),
            pltpu.VMEM((LAYERS, BD, 2 * BLOCK), jnp.float32),
            pltpu.VMEM((PIPE, OWN, ROWS + 8, 128), jnp.int32),
            pltpu.SMEM((PIPE, OWN, ROWS + 8, 128), jnp.int32),
            [[pltpu.VMEM((BD, rs, 128), jnp.bfloat16)] * SUBS] * LAYERS,
            [[pltpu.VMEM((2, BD, rs, 128), jnp.bfloat16)] * SUBS] * LAYERS,
            pltpu.VMEM((LAYERS, SUBS, 128, rs, 128), jnp.bfloat16),
            [[pltpu.VMEM((128, rs, 128), jnp.bfloat16)] * SUBS] * LAYERS,
            pltpu.SemaphoreType.DMA((1,)),
            pltpu.SemaphoreType.DMA((LAYERS,)),
            pltpu.SemaphoreType.DMA,
            pltpu.SemaphoreType.DMA((PIPE,)),
            pltpu.SemaphoreType.DMA,
            pltpu.SemaphoreType.DMA,
            pltpu.SemaphoreType.DMA,
            pltpu.SemaphoreType.DMA((LAYERS, CHUNKS)),
            pltpu.SemaphoreType.DMA((LAYERS, SUBS)),
            pltpu.SemaphoreType.DMA((LAYERS, SUBS)),
            pltpu.SemaphoreType.DMA((LAYERS, SUBS)),
            pltpu.SemaphoreType.DMA((LAYERS, SUBS)),
        ],
        compiler_params=pltpu.CompilerParams(
            collective_id=0, has_side_effects=True, vmem_limit_bytes=60 * 1024 * 1024
        ),
    )(features, weights, bias, layout)


def solution(mesh):
    in_specs = (
        P("pipe", "rows"),
        P("pipe", "rows", None, None),
        P("pipe", "rows"),
        P("pipe", None),
    )
    return jax.shard_map(
        on_device, mesh=mesh, in_specs=in_specs, out_specs=P("pipe", "rows"), check_vma=False
    )
```

```python
import functools

import jax
import jax.numpy as jnp
from jax import lax
from jax.experimental import pallas as pl
from jax.experimental.pallas import tpu as pltpu
from jax.sharding import PartitionSpec as P

MESH = pl.DeviceIdType.MESH
BLOCK = 64
K = 4
X, Z, C = 4, 8, 2
PIPE = 4
ROWS = X * Z * C
LAYERS = 8
OWN = LAYERS // PIPE
BD = 16
SUBS = 4
LAG = 1
CHUNKS = 4
clamp_top = 32.0

OWN_PARTS = ((6, 1, (0,)), (10, -1, (0,)), (0, 0, (0,)))
RELAY_PARTS = ((8, 1, (1,)), (12, -1, (2,)), (2, 0, (1, 2)))
HERE = 6


def place():
    me = lax.axis_index("rows")
    return lax.axis_index("pipe"), me >> 4, (me >> 1) & (Z - 1), me & (C - 1)


def device(dy, dx, dz, dc):
    y, x, z, c = place()
    row = (((x + dx) & (X - 1)) << 4) | (((z + dz) & (Z - 1)) << 1) | ((c ^ dc) & (C - 1))
    return ((y + dy) & (PIPE - 1), row)


def offsets():
    found = [(1, 0, 0, 0), (2, 0, 0, 0), (3, 0, 0, 0), (0, 0, 2, 0), (0, 0, -2, 0)]
    for dx in range(X):
        for dc in range(C):
            for dz in (0, 1, -1, 2 if dc == 0 else -2):
                here = (0, dx, dz, dc)
                if here not in found and here != (0, 0, 0, 0):
                    found.append(here)
    return found


def swap_halves(v):
    return pltpu.roll(v, BLOCK, 1)


def kernel(
    feat_ref, w_hbm, bias_ref, lay_ref, out_ref,
    wall, ready, biases, bias_tiles, tabs, stab, cur, near, stage, land,
    local_sem, smem_sem, tab_send, tab_recv, bias_send, bias_recv, w_send, w_recv,
    hop_send, hop_recv, leaf_send, leaf_recv,
):
    y, x, z, c = place()
    me = (x * Z + z) * C + c
    rs = cur[0][0].shape[1]
    left = lax.broadcasted_iota(jnp.int32, (BD, 128), 1) < BLOCK

    barrier = pltpu.get_barrier_semaphore()
    partners = offsets()
    for dy, dx, dz, dc in partners:
        pl.semaphore_signal(
            barrier, inc=1, device_id=device(-dy, -dx, -dz, -dc), device_id_type=MESH
        )

    own_w = pltpu.make_async_copy(w_hbm, wall.at[pl.ds(OWN * y, OWN)], local_sem.at[0])
    own_w.start()

    def fold(p, carry):
        cols = pl.ds(pl.multiple_of(p * 128, 128), 128)
        low = feat_ref[pl.ds(0, 16), cols].astype(jnp.float32)
        high = feat_ref[pl.ds(16, 16), cols].astype(jnp.float32)
        even = jnp.where(left, low, swap_halves(high)).astype(jnp.bfloat16)
        odd = jnp.where(left, swap_halves(low), high).astype(jnp.bfloat16)
        for s in range(SUBS):
            cur[0][s][2 * p] = even[s * rs : (s + 1) * rs]
            cur[0][s][2 * p + 1] = odd[s * rs : (s + 1) * rs]
        return carry

    lax.fori_loop(0, BD // 2, fold, 0)
    biases[pl.ds(y, 1)] = bias_ref[...].reshape(1, OWN, bias_ref.shape[1])

    lane = lax.broadcasted_iota(jnp.int32, (ROWS // 2, 128), 1)
    slot = lane & 63
    for a in range(OWN):
        entry = jnp.concatenate(
            [lay_ref[pl.ds(a, 1), pl.ds(i * 128, 128)] for i in range(ROWS // 2)], axis=0
        )
        owner = entry >> 4
        key = slot * BD + (entry & 15)
        for half in range(2):
            table = jnp.zeros((ROWS // 2, 128), jnp.int32)
            for q, dz in enumerate((0, -2, 2)):
                source = (x << 4) | (((z + dz) & (Z - 1)) << 1) | c
                hit = (owner == source) & ((lane >> 6) == half)
                first = jnp.min(jnp.where(hit, key, 1 << 20), axis=1, keepdims=True) & 15
                last = jnp.max(jnp.where(hit, key, 0), axis=1, keepdims=True) & 15
                table = jnp.where(lane == 2 * q, first, table)
                table = jnp.where(lane == 2 * q + 1, last, table)
            tabs[y, a, pl.ds(half * ROWS // 2, ROWS // 2)] = table
    mine = jnp.concatenate(
        [lay_ref[:, pl.ds(pl.multiple_of((x * Z + z) * 128, 128), 128)]]
        + [jnp.zeros((8 - OWN, 128), jnp.int32)],
        axis=0,
    )
    owner = mine >> 4
    spot = lax.broadcasted_iota(jnp.int32, (8, 128), 1) & 63
    rank = jnp.zeros((8, 128), jnp.int32)
    for step in range(1, 64):
        same = (pltpu.roll(owner, step, 1) == owner) & (spot >= step)
        rank = jnp.where(same, 1, rank)
    dx = (x - (owner >> 4) + X) & (X - 1)
    dz = (z - ((owner >> 1) & (Z - 1)) + Z) & (Z - 1)
    dc = (c + owner) & 1
    base = jnp.zeros((8, 128), jnp.int32)
    for d, at in ((0, 0), (2, 2), (6, 4), (1, 6), (3, 8), (7, 10), (5, 12), (4, 14)):
        base = jnp.where(dz == d, at, base)
    where = (dx * 2 + dc) * 16 + base + rank
    for a in range(OWN):
        both_rows = jnp.concatenate(
            [where[a : a + 1], pltpu.roll(where, 64, 1)[a : a + 1], jnp.zeros((6, 128), jnp.int32)], axis=0
        )
        tabs[y, a, pl.ds(ROWS, 8)] = both_rows

    own_w.wait()
    with jax.named_scope("barrier_wait"):
        pl.semaphore_wait(barrier, len(partners))

    def tab_copy(a, dy):
        return pltpu.make_async_remote_copy(
            tabs.at[y, a], tabs.at[y, a], tab_send, tab_recv.at[y, a],
            device_id=device(dy, 0, 0, 0), device_id_type=MESH,
        )

    def bias_copy(dy):
        return pltpu.make_async_remote_copy(
            biases.at[y], biases.at[y], bias_send, bias_recv,
            device_id=device(dy, 0, 0, 0), device_id_type=MESH,
        )

    def hop(l, s, dz, q):
        return pltpu.make_async_remote_copy(
            cur[l][s], near[l][s].at[q], hop_send.at[l, s], hop_recv.at[l, s],
            device_id=device(0, 0, dz, 0), device_id_type=MESH,
        )

    def start_hops(l, s):
        hop(l, s, 2, 0).start()
        hop(l, s, -2, 1).start()

    rows = BD // CHUNKS

    def w_copy(l, chunk, dy, src):
        piece = pl.ds(chunk * rows, rows)
        return pltpu.make_async_remote_copy(
            src.at[piece], wall.at[l, piece], w_send, w_recv.at[l, chunk],
            device_id=device(dy, 0, 0, 0), device_id_type=MESH,
        )

    def w_own(a, dy, order):
        for chunk in order:
            w_copy(OWN * y + a, chunk, dy, wall.at[OWN * y + a]).start()

    def w_wait(l, order):
        for chunk in order:
            w_copy(l, chunk, 1, wall.at[l]).wait_recv()

    def w_pass(l, order, dy):
        for chunk in order:
            w_wait(l, (chunk,))
            w_copy(l, chunk, dy, wall.at[l]).start()

    def at_y(which, act):
        pl.when(y == which)(act)


    h1, h2 = (0, 1), (2, 3)

    def own(which, *ways):
        return tuple(
            ("own", which, dy, chunks or (h1 + h2 if dy > 0 else h2 + h1)) for dy, chunks in ways
        )

    def fwd(l, dy, chunks):
        return (("pass", l, dy, chunks),)

    up, down = (1, None), (-1, None)
    program = {
        "start": (
            (0, own(0, up, down)),
            (1, own(0, down) + own(1, down)),
            (2, own(0, down) + own(1, down)),
            (3, own(0, up) + own(1, up)),
        ),
        "first": ((1, fwd(0, 1, h1) + own(0, (1, h1))), (3, fwd(0, -1, h2))),
        (0, 0): ((0, own(1, up, down)), (1, fwd(1, 1, (0,))), (3, fwd(1, -1, (2,)))),
        (0, 1): (
            (1, fwd(1, 1, (1,)) + own(0, (1, h2)) + own(1, up)),
            (3, fwd(1, -1, (3,)) + own(0, down) + own(1, down)),
        ),
        (0, 2): ((2, fwd(2, 1, h1) + own(0, up)),),
        (0, 3): ((0, fwd(2, -1, h2)),),
        (1, 0): ((0, fwd(3, -1, h2)), (1, fwd(4, -1, h1 + h2) + fwd(5, -1, h1 + h2))),
        (2, 0): ((2, fwd(3, 1, h1) + own(1, up)),),
        (2, 1): ((0, fwd(6, 1, h1) + fwd(7, 1, h1)), (2, fwd(6, -1, h2))),
        (3, 0): ((2, fwd(7, -1, h2)),),
    }

    def acts_of(who):
        return [act for step in program.values() for y_at, acts in step if y_at == who for act in acts]

    def point(*at):
        for who, acts in program.get(at if len(at) > 1 else at[0], ()):
            @functools.partial(at_y, who)
            def _():
                for kind, which, dy, order in acts:
                    if kind == "own":
                        w_own(which, dy, order)
                    else:
                        w_pass(which, order, dy)

    def arrive(l):
        owner = l // OWN
        for who in range(PIPE):
            passed = [
                chunk
                for kind, which, _, order in acts_of(who) if kind == "pass" and which == l
                for chunk in order
            ]
            order = tuple(chunk for chunk in h1 + h2 if chunk not in passed)
            if who != owner and order:
                at_y(who, functools.partial(w_wait, l, order))

    def prepare(l):
        keep = lax.broadcasted_iota(jnp.int32, (BLOCK, 128), 1) < BLOCK

        def one(r, carry):
            for p in range(2):
                raw = wall[l, r, :, pl.ds(p * 128, 128)].astype(jnp.float32)
                turn = swap_halves(raw)
                zero = jnp.zeros_like(raw)
                parts = (
                    jnp.where(keep, raw, zero), jnp.where(keep, zero, turn),
                    jnp.where(keep, turn, zero), jnp.where(keep, zero, raw),
                )
                for i, part in enumerate(parts):
                    ready[l, r, pl.ds((p * 4 + i) * BLOCK, BLOCK), :] = part.astype(jnp.bfloat16)
            return carry

        lax.fori_loop(0, BD, one, 0, unroll=4)

        line_left = lax.broadcasted_iota(jnp.int32, (1, 128), 1) < BLOCK

        for p in range(BD // 2):
            row = biases[l // OWN, pl.ds(l % OWN, 1), pl.ds(p * 128, 128)].astype(jnp.float32)
            turn = swap_halves(row)
            bias_tiles[l, pl.ds(2 * p, 1), :] = jnp.where(line_left, row, turn)
            bias_tiles[l, pl.ds(2 * p + 1, 1), :] = jnp.where(line_left, turn, row)

    def leaf(l, s, base, dx, dz, dc, at, n):
        tiles = pl.ds(base + at, n)
        return pltpu.make_async_remote_copy(
            stage.at[l, s, tiles], land[l][s].at[tiles], leaf_send.at[l, s], leaf_recv.at[l, s],
            device_id=device(0, dx, dz, dc), device_id_type=MESH,
        )

    def hop_wait(l, s):
        pltpu.make_async_remote_copy(
            near[l][s], near[l][s], hop_send.at[l, s], hop_recv.at[l, s],
            device_id=device(0, 0, 2, 0), device_id_type=MESH,
        ).wait_recv()

    def columns(l, s, parts, far):
        def column(t, carry):
            dx = t ^ 2
            xx = ((x + dx) & (X - 1)) << 3
            plans = []
            for dc in range(C):
                todo = parts
                if far:
                    todo = ((14, 2 - 4 * dc, (1 + dc,)),) + parts
                plans.append((dc, (dx * 2 + dc) * 16, todo))
            moves = []
            for dc, base, todo in plans:
                for at, dz, sources in todo:
                    row = ((c ^ dc) << 5) | xx | ((z + dz) & (Z - 1))
                    for i, q in enumerate(sources):
                        for k in range(2):
                            index = stab[l // OWN, l % OWN, row, 2 * q + k]
                            moves.append((base + at + 2 * i + k, q, index))
            tiles = [near[l][s][q - 1, i] if far else cur[l][s][i] for _, q, i in moves]
            for (at, _, _), tile in zip(moves, tiles):
                stage[l, s, at] = tile
            for dc, base, todo in plans:
                for at, dz, sources in todo:
                    go = leaf(l, s, base, dx, dz, dc, at, 2 * len(sources))
                    if dz == 0 and dc == 0:
                        pl.when(dx > 0)(go.start)
                    else:
                        go.start()
            return carry

        lax.fori_loop(0, X, column, 0)
        for at, dz, sources in parts:
            if dz == 0:
                for k in range(at, at + 2 * len(sources)):
                    land[l][s][k] = stage[l, s, k]

    def pack_own(l, s):
        columns(l, s, OWN_PARTS, False)

    def pack(l, s):
        columns(l, s, RELAY_PARTS, True)

    def spread(l, s):
        hop_wait(l, s)
        pack(l, s)

    def gather(l, s):
        tiles = pl.ds(HERE, 8 * 16 - HERE)
        pltpu.make_async_remote_copy(
            stage.at[l, s, tiles], land[l][s].at[tiles], leaf_send.at[l, s], leaf_recv.at[l, s],
            device_id=device(0, 1, 0, 0), device_id_type=MESH,
        ).wait_recv()

    def block_out(l, s, r):
        row = stab.at[l // OWN, l % OWN, ROWS + c]
        lhs = jnp.concatenate([land[l][s][row[r * K + k]] for k in range(K)], axis=1)
        total = jnp.dot(lhs, ready[l, r], preferred_element_type=jnp.float32)
        total = total + bias_tiles[l, pl.ds(r, 1), :]
        return jnp.minimum(jnp.maximum(total, 0.0), clamp_top)

    def advance(l, s):
        gather(l, s)
        compute(l, s)
        start_hops(l + 1, s)
        pack_own(l + 1, s)

    def compute(l, s):
        def pair(p, carry):
            for r in range(2):
                cur[l + 1][s][2 * p + r] = block_out(l, s, 2 * p + r).astype(jnp.bfloat16)
            return carry

        lax.fori_loop(0, BD // 2, pair, 0, unroll=8)

    def finish(l, s):
        gather(l, s)
        finish_compute(l, s)

    def finish_compute(l, s):
        half = left[:rs]

        def pair(p, carry):
            even, odd = block_out(l, s, 2 * p), block_out(l, s, 2 * p + 1)
            cols = pl.ds(pl.multiple_of(p * 128, 128), 128)
            low = jnp.where(half, even, swap_halves(odd))
            high = jnp.where(half, swap_halves(even), odd)
            out_ref[pl.ds(s * rs, rs), cols] = low.astype(jnp.bfloat16)
            out_ref[pl.ds(16 + s * rs, rs), cols] = high.astype(jnp.bfloat16)
            return carry

        lax.fori_loop(0, BD // 2, pair, 0, unroll=8)

    def tab_wait(l):
        @pl.when(y != l // OWN)
        def _():
            at = (l // OWN, l % OWN)
            pltpu.make_async_remote_copy(
                tabs.at[at], tabs.at[at], tab_send, tab_recv.at[at],
                device_id=device(1, 0, 0, 0), device_id_type=MESH,
            ).wait_recv()

    def to_smem(l):
        at = (l // OWN, l % OWN)
        return pltpu.make_async_copy(tabs.at[at], stab.at[at], smem_sem.at[l])

    def smem_wait(l):
        to_smem(l).wait()

    for dy in (2, 1, 3):
        tab_copy(0, dy).start()
    for s in range(SUBS):
        start_hops(0, s)
    for dy in (2, 1, 3):
        tab_copy(1, dy).start()
    for dy in (1, 2, 3):
        bias_copy(dy).start()
    point("start")
    tab_wait(0)
    to_smem(0).start()
    smem_wait(0)
    for s in range(SUBS):
        pack_own(0, s)
    for s in range(SUBS):
        spread(0, s)
    for l in range(1, LAYERS):
        tab_wait(l)
        to_smem(l).start()
    pltpu.make_async_remote_copy(
        biases.at[pl.ds(0, 3)], biases.at[pl.ds(0, 3)], bias_send, bias_recv,
        device_id=device(1, 0, 0, 0), device_id_type=MESH,
    ).wait()
    point("first")
    arrive(0)
    prepare(0)
    last = LAYERS - 1
    order = [(l, s) for l in range(LAYERS) for s in range(SUBS)]
    for n, (l, s) in enumerate(order):
        if s == 0 and l < last:
            smem_wait(l + 1)
        if l < last:
            advance(l, s)
        else:
            finish(l, s)
        point(l, s)
        if s == SUBS - 1 and 0 < l < last:
            arrive(l + 1)
            prepare(l + 1)
        if n >= LAG:
            behind_l, behind_s = order[n - LAG]
            if behind_l < last:
                spread(behind_l + 1, behind_s)
        if s == SUBS - 1 and l == 0:
            arrive(l + 1)
            prepare(l + 1)

    pltpu.make_async_remote_copy(
        tabs.at[pl.ds(0, 3)], tabs.at[pl.ds(0, 3)], tab_send, tab_recv.at[0, 0],
        device_id=device(1, 0, 0, 0), device_id_type=MESH,
    ).wait_send()
    for l in range(LAYERS):
        for s in range(SUBS):
            pltpu.make_async_remote_copy(
                near[l][s], near[l][s], hop_send.at[l, s], hop_recv.at[l, s],
                device_id=device(0, 0, 2, 0), device_id_type=MESH,
            ).wait_send()
            tiles = pl.ds(HERE, 8 * 16 - HERE)
            pltpu.make_async_remote_copy(
                stage.at[l, s, tiles], land[l][s].at[tiles], leaf_send.at[l, s], leaf_recv.at[l, s],
                device_id=device(0, 1, 0, 0), device_id_type=MESH,
            ).wait_send()
    for who in range(PIPE):
        pieces = sum(len(order) for _, _, _, order in acts_of(who))

        @functools.partial(at_y, who)
        def _():
            pltpu.make_async_remote_copy(
                wall.at[:, pl.ds(0, pieces * rows // LAYERS)],
                wall.at[:, pl.ds(0, pieces * rows // LAYERS)],
                w_send, w_recv.at[0, 0],
                device_id=device(1, 0, 0, 0), device_id_type=MESH,
            ).wait_send()


def on_device(features, weights, bias, layout):
    rs = 16 // SUBS
    n = bias.shape[1]
    return pl.pallas_call(
        kernel,
        name="sections",
        out_shape=jax.ShapeDtypeStruct(features.shape, jnp.bfloat16),
        in_specs=[
            pl.BlockSpec(memory_space=pltpu.VMEM),
            pl.BlockSpec(memory_space=pl.ANY),
            pl.BlockSpec(memory_space=pltpu.VMEM),
            pl.BlockSpec(memory_space=pltpu.VMEM),
        ],
        out_specs=pl.BlockSpec(memory_space=pltpu.VMEM),
        scratch_shapes=[
            pltpu.VMEM((LAYERS,) + weights.shape[1:], jnp.bfloat16),
            pltpu.VMEM((LAYERS, BD, 2 * K * BLOCK, 2 * BLOCK), jnp.bfloat16),
            pltpu.VMEM((PIPE, OWN, n), jnp.bfloat16),
            pltpu.VMEM((LAYERS, BD, 2 * BLOCK), jnp.float32),
            pltpu.VMEM((PIPE, OWN, ROWS + 8, 128), jnp.int32),
            pltpu.SMEM((PIPE, OWN, ROWS + 8, 128), jnp.int32),
            [[pltpu.VMEM((BD, rs, 128), jnp.bfloat16)] * SUBS] * LAYERS,
            [[pltpu.VMEM((2, BD, rs, 128), jnp.bfloat16)] * SUBS] * LAYERS,
            pltpu.VMEM((LAYERS, SUBS, 128, rs, 128), jnp.bfloat16),
            [[pltpu.VMEM((128, rs, 128), jnp.bfloat16)] * SUBS] * LAYERS,
            pltpu.SemaphoreType.DMA((1,)),
            pltpu.SemaphoreType.DMA((LAYERS,)),
            pltpu.SemaphoreType.DMA,
            pltpu.SemaphoreType.DMA((PIPE, OWN)),
            pltpu.SemaphoreType.DMA,
            pltpu.SemaphoreType.DMA,
            pltpu.SemaphoreType.DMA,
            pltpu.SemaphoreType.DMA((LAYERS, CHUNKS)),
            pltpu.SemaphoreType.DMA((LAYERS, SUBS)),
            pltpu.SemaphoreType.DMA((LAYERS, SUBS)),
            pltpu.SemaphoreType.DMA((LAYERS, SUBS)),
            pltpu.SemaphoreType.DMA((LAYERS, SUBS)),
        ],
        compiler_params=pltpu.CompilerParams(
            collective_id=0, has_side_effects=True, vmem_limit_bytes=60 * 1024 * 1024
        ),
    )(features, weights, bias, layout)


def solution(mesh):
    in_specs = (
        P("pipe", "rows"),
        P("pipe", "rows", None, None),
        P("pipe", "rows"),
        P("pipe", None),
    )
    return jax.shard_map(
        on_device, mesh=mesh, in_specs=in_specs, out_specs=P("pipe", "rows"), check_vma=False
    )
```

```python
import functools

import jax
import jax.numpy as jnp
from jax import lax
from jax.experimental import pallas as pl
from jax.experimental.pallas import tpu as pltpu
from jax.sharding import PartitionSpec as P

MESH = pl.DeviceIdType.MESH
BLOCK = 64
K = 4
X, Z, C = 4, 8, 2
PIPE = 4
ROWS = X * Z * C
LAYERS = 8
OWN = LAYERS // PIPE
BD = 16
SUBS = 4
CHUNKS = 4
clamp_top = 32.0

OWN_PARTS = ((6, 1, (0,)), (10, -1, (0,)), (0, 0, (0,)))
RELAY_PARTS = ((8, 1, (1,)), (12, -1, (2,)), (2, 0, (1, 2)))
HERE = 6


def place():
    me = lax.axis_index("rows")
    return lax.axis_index("pipe"), me >> 4, (me >> 1) & (Z - 1), me & (C - 1)


def device(dy, dx, dz, dc):
    y, x, z, c = place()
    row = (((x + dx) & (X - 1)) << 4) | (((z + dz) & (Z - 1)) << 1) | ((c ^ dc) & (C - 1))
    return ((y + dy) & (PIPE - 1), row)


def offsets():
    found = [(1, 0, 0, 0), (2, 0, 0, 0), (3, 0, 0, 0), (0, 0, 2, 0), (0, 0, -2, 0)]
    for dx in range(X):
        for dc in range(C):
            for dz in (0, 1, -1, 2 if dc == 0 else -2):
                here = (0, dx, dz, dc)
                if here not in found and here != (0, 0, 0, 0):
                    found.append(here)
    return found


def swap_halves(v):
    return pltpu.roll(v, BLOCK, 1)


def kernel(
    feat_ref, w_hbm, bias_ref, lay_ref, out_ref,
    wall, ready, biases, bias_tiles, tabs, stab, cur, near, stage, land,
    local_sem, smem_sem, tab_send, tab_recv, bias_send, bias_recv, w_send, w_recv,
    hop_send, hop_recv, leaf_send, leaf_recv,
):
    y, x, z, c = place()
    me = (x * Z + z) * C + c
    rs = cur[0][0].shape[1]
    left = lax.broadcasted_iota(jnp.int32, (BD, 128), 1) < BLOCK

    barrier = pltpu.get_barrier_semaphore()
    partners = offsets()
    for dy, dx, dz, dc in partners:
        pl.semaphore_signal(
            barrier, inc=1, device_id=device(-dy, -dx, -dz, -dc), device_id_type=MESH
        )

    own_w = pltpu.make_async_copy(w_hbm, wall.at[pl.ds(OWN * y, OWN)], local_sem.at[0])
    own_w.start()

    def fold(p, carry):
        cols = pl.ds(pl.multiple_of(p * 128, 128), 128)
        low = feat_ref[pl.ds(0, 16), cols].astype(jnp.float32)
        high = feat_ref[pl.ds(16, 16), cols].astype(jnp.float32)
        even = jnp.where(left, low, swap_halves(high)).astype(jnp.bfloat16)
        odd = jnp.where(left, swap_halves(low), high).astype(jnp.bfloat16)
        for s in range(SUBS):
            cur[0][s][2 * p] = even[s * rs : (s + 1) * rs]
            cur[0][s][2 * p + 1] = odd[s * rs : (s + 1) * rs]
        return carry

    lax.fori_loop(0, BD // 2, fold, 0)
    biases[pl.ds(y, 1)] = bias_ref[...].reshape(1, OWN, bias_ref.shape[1])

    lane = lax.broadcasted_iota(jnp.int32, (ROWS // 2, 128), 1)
    slot = lane & 63
    for a in range(OWN):
        entry = jnp.concatenate(
            [lay_ref[pl.ds(a, 1), pl.ds(i * 128, 128)] for i in range(ROWS // 2)], axis=0
        )
        owner = entry >> 4
        key = slot * BD + (entry & 15)
        for half in range(2):
            table = jnp.zeros((ROWS // 2, 128), jnp.int32)
            for q, dz in enumerate((0, -2, 2)):
                source = (x << 4) | (((z + dz) & (Z - 1)) << 1) | c
                hit = (owner == source) & ((lane >> 6) == half)
                first = jnp.min(jnp.where(hit, key, 1 << 20), axis=1, keepdims=True) & 15
                last = jnp.max(jnp.where(hit, key, 0), axis=1, keepdims=True) & 15
                table = jnp.where(lane == 2 * q, first, table)
                table = jnp.where(lane == 2 * q + 1, last, table)
            tabs[y, a, pl.ds(half * ROWS // 2, ROWS // 2)] = table
    mine = jnp.concatenate(
        [lay_ref[:, pl.ds(pl.multiple_of((x * Z + z) * 128, 128), 128)]]
        + [jnp.zeros((8 - OWN, 128), jnp.int32)],
        axis=0,
    )
    owner = mine >> 4
    spot = lax.broadcasted_iota(jnp.int32, (8, 128), 1) & 63
    rank = jnp.zeros((8, 128), jnp.int32)
    for step in range(1, 64):
        same = (pltpu.roll(owner, step, 1) == owner) & (spot >= step)
        rank = jnp.where(same, 1, rank)
    dx = (x - (owner >> 4) + X) & (X - 1)
    dz = (z - ((owner >> 1) & (Z - 1)) + Z) & (Z - 1)
    dc = (c + owner) & 1
    base = jnp.zeros((8, 128), jnp.int32)
    for d, at in ((0, 0), (2, 2), (6, 4), (1, 6), (3, 8), (7, 10), (5, 12), (4, 14)):
        base = jnp.where(dz == d, at, base)
    where = (dx * 2 + dc) * 16 + base + rank
    for a in range(OWN):
        both_rows = jnp.concatenate(
            [where[a : a + 1], pltpu.roll(where, 64, 1)[a : a + 1], jnp.zeros((6, 128), jnp.int32)], axis=0
        )
        tabs[y, a, pl.ds(ROWS, 8)] = both_rows

    own_w.wait()
    with jax.named_scope("barrier_wait"):
        pl.semaphore_wait(barrier, len(partners))

    def tab_copy(a, dy):
        return pltpu.make_async_remote_copy(
            tabs.at[y, a], tabs.at[y, a], tab_send, tab_recv.at[y, a],
            device_id=device(dy, 0, 0, 0), device_id_type=MESH,
        )

    def bias_copy(dy):
        return pltpu.make_async_remote_copy(
            biases.at[y], biases.at[y], bias_send, bias_recv,
            device_id=device(dy, 0, 0, 0), device_id_type=MESH,
        )

    def hop(l, s, dz, q):
        return pltpu.make_async_remote_copy(
            cur[l][s], near[l][s].at[q], hop_send.at[l, s], hop_recv.at[l, s],
            device_id=device(0, 0, dz, 0), device_id_type=MESH,
        )

    def start_hops(l, s):
        hop(l, s, 2, 0).start()
        hop(l, s, -2, 1).start()

    rows = BD // CHUNKS

    def w_copy(l, chunk, dy, src):
        piece = pl.ds(chunk * rows, rows)
        return pltpu.make_async_remote_copy(
            src.at[piece], wall.at[l, piece], w_send, w_recv.at[l, chunk],
            device_id=device(dy, 0, 0, 0), device_id_type=MESH,
        )

    def w_own(a, dy, order):
        for chunk in order:
            w_copy(OWN * y + a, chunk, dy, wall.at[OWN * y + a]).start()

    def w_wait(l, order):
        for chunk in order:
            w_copy(l, chunk, 1, wall.at[l]).wait_recv()

    def w_pass(l, order, dy):
        for chunk in order:
            w_wait(l, (chunk,))
            w_copy(l, chunk, dy, wall.at[l]).start()

    def at_y(which, act):
        pl.when(y == which)(act)


    h1, h2 = (0, 1), (2, 3)

    def own(which, *ways):
        return tuple(
            ("own", which, dy, chunks or (h1 + h2 if dy > 0 else h2 + h1)) for dy, chunks in ways
        )

    def fwd(l, dy, chunks):
        return (("pass", l, dy, chunks),)

    up, down = (1, None), (-1, None)
    program = {
        "start": (
            (0, own(0, up, down)),
            (1, own(0, down) + own(1, down)),
            (2, own(0, down) + own(1, down)),
            (3, own(0, up) + own(1, up)),
        ),
        "first": (
            (0, own(1, up, down)),
            (1, fwd(0, 1, h1) + own(0, (1, h1))),
            (3, fwd(0, -1, h2)),
        ),
        (0, 0): ((1, fwd(1, 1, (0,))), (3, fwd(1, -1, (2,)))),
        (0, 1): (
            (1, fwd(1, 1, (1,)) + own(0, (1, h2)) + own(1, up)),
            (3, fwd(1, -1, (3,)) + own(0, down) + own(1, down)),
        ),
        (0, 2): ((2, fwd(2, 1, h1) + own(0, (1, h1))),),
        (0, 3): ((0, fwd(2, -1, h2)),),
        (1, 0): ((0, fwd(3, -1, h2)), (1, fwd(4, -1, h1 + h2) + fwd(5, -1, h1 + h2))),
        (1, 3): ((2, fwd(3, 1, (0,))),),
        (2, 0): ((2, fwd(3, 1, (1,)) + own(0, (1, h2))),),
        (2, 1): ((0, fwd(6, 1, h1) + fwd(7, 1, h1)), (2, own(1, up) + fwd(6, -1, h2))),
        (3, 0): ((2, fwd(7, -1, h2)),),
    }

    def acts_of(who):
        return [act for step in program.values() for y_at, acts in step if y_at == who for act in acts]

    def point(*at):
        for who, acts in program.get(at if len(at) > 1 else at[0], ()):
            @functools.partial(at_y, who)
            def _():
                for kind, which, dy, order in acts:
                    if kind == "own":
                        w_own(which, dy, order)
                    else:
                        w_pass(which, order, dy)

    def arrive(l):
        owner = l // OWN
        for who in range(PIPE):
            passed = [
                chunk
                for kind, which, _, order in acts_of(who) if kind == "pass" and which == l
                for chunk in order
            ]
            order = tuple(chunk for chunk in h1 + h2 if chunk not in passed)
            if who != owner and order:
                at_y(who, functools.partial(w_wait, l, order))

    def prepare(l):
        keep = lax.broadcasted_iota(jnp.int32, (BLOCK, 128), 1) < BLOCK

        def one(r, carry):
            for p in range(2):
                raw = wall[l, r, :, pl.ds(p * 128, 128)].astype(jnp.float32)
                turn = swap_halves(raw)
                zero = jnp.zeros_like(raw)
                parts = (
                    jnp.where(keep, raw, zero), jnp.where(keep, zero, turn),
                    jnp.where(keep, turn, zero), jnp.where(keep, zero, raw),
                )
                for i, part in enumerate(parts):
                    ready[l, r, pl.ds((p * 4 + i) * BLOCK, BLOCK), :] = part.astype(jnp.bfloat16)
            return carry

        lax.fori_loop(0, BD, one, 0, unroll=4)

        line_left = lax.broadcasted_iota(jnp.int32, (1, 128), 1) < BLOCK

        for p in range(BD // 2):
            row = biases[l // OWN, pl.ds(l % OWN, 1), pl.ds(p * 128, 128)].astype(jnp.float32)
            turn = swap_halves(row)
            bias_tiles[l, pl.ds(2 * p, 1), :] = jnp.where(line_left, row, turn)
            bias_tiles[l, pl.ds(2 * p + 1, 1), :] = jnp.where(line_left, turn, row)

    def leaf(l, s, base, dx, dz, dc, at, n):
        tiles = pl.ds(base + at, n)
        return pltpu.make_async_remote_copy(
            stage.at[l, s, tiles], land[l][s].at[tiles], leaf_send.at[l, s], leaf_recv.at[l, s],
            device_id=device(0, dx, dz, dc), device_id_type=MESH,
        )

    def hop_wait(l, s):
        pltpu.make_async_remote_copy(
            near[l][s], near[l][s], hop_send.at[l, s], hop_recv.at[l, s],
            device_id=device(0, 0, 2, 0), device_id_type=MESH,
        ).wait_recv()

    def columns(l, s, parts, far):
        def column(t, carry):
            dx = t ^ 2
            xx = ((x + dx) & (X - 1)) << 3
            plans = []
            for dc in range(C):
                todo = parts
                if far:
                    todo = ((14, 2 - 4 * dc, (1 + dc,)),) + parts
                plans.append((dc, (dx * 2 + dc) * 16, todo))
            moves = []
            for dc, base, todo in plans:
                for at, dz, sources in todo:
                    row = ((c ^ dc) << 5) | xx | ((z + dz) & (Z - 1))
                    for i, q in enumerate(sources):
                        for k in range(2):
                            index = stab[l // OWN, l % OWN, row, 2 * q + k]
                            moves.append((base + at + 2 * i + k, q, index))
            tiles = [near[l][s][q - 1, i] if far else cur[l][s][i] for _, q, i in moves]
            for (at, _, _), tile in zip(moves, tiles):
                stage[l, s, at] = tile
            for dc, base, todo in plans:
                for at, dz, sources in todo:
                    go = leaf(l, s, base, dx, dz, dc, at, 2 * len(sources))
                    if dz == 0 and dc == 0:
                        pl.when(dx > 0)(go.start)
                    else:
                        go.start()
            return carry

        lax.fori_loop(0, X, column, 0)
        for at, dz, sources in parts:
            if dz == 0:
                for k in range(at, at + 2 * len(sources)):
                    land[l][s][k] = stage[l, s, k]

    def pack_own(l, s):
        columns(l, s, OWN_PARTS, False)

    def pack(l, s):
        columns(l, s, RELAY_PARTS, True)

    def spread(l, s):
        hop_wait(l, s)
        pack(l, s)

    def gather(l, s):
        tiles = pl.ds(HERE, 8 * 16 - HERE)
        pltpu.make_async_remote_copy(
            stage.at[l, s, tiles], land[l][s].at[tiles], leaf_send.at[l, s], leaf_recv.at[l, s],
            device_id=device(0, 1, 0, 0), device_id_type=MESH,
        ).wait_recv()

    def block_out(l, s, r):
        row = stab.at[l // OWN, l % OWN, ROWS + c]
        lhs = jnp.concatenate([land[l][s][row[r * K + k]] for k in range(K)], axis=1)
        total = jnp.dot(lhs, ready[l, r], preferred_element_type=jnp.float32)
        total = total + bias_tiles[l, pl.ds(r, 1), :]
        return jnp.minimum(jnp.maximum(total, 0.0), clamp_top)

    def advance(l, s):
        gather(l, s)
        compute(l, s)
        start_hops(l + 1, s)
        pack_own(l + 1, s)

    def compute(l, s):
        def pair(p, carry):
            for r in range(2):
                cur[l + 1][s][2 * p + r] = block_out(l, s, 2 * p + r).astype(jnp.bfloat16)
            return carry

        lax.fori_loop(0, BD // 2, pair, 0, unroll=8)

    def finish(l, s):
        gather(l, s)
        finish_compute(l, s)

    def finish_compute(l, s):
        half = left[:rs]

        def pair(p, carry):
            even, odd = block_out(l, s, 2 * p), block_out(l, s, 2 * p + 1)
            cols = pl.ds(pl.multiple_of(p * 128, 128), 128)
            low = jnp.where(half, even, swap_halves(odd))
            high = jnp.where(half, swap_halves(even), odd)
            out_ref[pl.ds(s * rs, rs), cols] = low.astype(jnp.bfloat16)
            out_ref[pl.ds(16 + s * rs, rs), cols] = high.astype(jnp.bfloat16)
            return carry

        lax.fori_loop(0, BD // 2, pair, 0, unroll=8)

    def tab_wait(l):
        @pl.when(y != l // OWN)
        def _():
            at = (l // OWN, l % OWN)
            pltpu.make_async_remote_copy(
                tabs.at[at], tabs.at[at], tab_send, tab_recv.at[at],
                device_id=device(1, 0, 0, 0), device_id_type=MESH,
            ).wait_recv()

    def to_smem(l):
        at = (l // OWN, l % OWN)
        return pltpu.make_async_copy(tabs.at[at], stab.at[at], smem_sem.at[l])

    def smem_wait(l):
        to_smem(l).wait()

    for dy in (2, 1, 3):
        tab_copy(0, dy).start()
    for s in range(SUBS):
        start_hops(0, s)
    for dy in (2, 1, 3):
        tab_copy(1, dy).start()
    for dy in (1, 2, 3):
        bias_copy(dy).start()
    point("start")
    tab_wait(0)
    to_smem(0).start()
    smem_wait(0)
    for s in range(SUBS):
        pack_own(0, s)
    for s in range(SUBS):
        spread(0, s)
    for l in range(1, LAYERS):
        tab_wait(l)
        to_smem(l).start()
    pltpu.make_async_remote_copy(
        biases.at[pl.ds(0, 3)], biases.at[pl.ds(0, 3)], bias_send, bias_recv,
        device_id=device(1, 0, 0, 0), device_id_type=MESH,
    ).wait()
    point("first")
    arrive(0)
    prepare(0)
    last = LAYERS - 1
    for l in range(LAYERS):
        if l == last:
            for s in range(SUBS):
                finish(l, s)
            break
        smem_wait(l + 1)
        for s in range(SUBS):
            advance(l, s)
        point(l, 0)
        point(l, 1)
        for s in range(SUBS):
            spread(l + 1, s)
        point(l, 2)
        point(l, 3)
        arrive(l + 1)
        prepare(l + 1)

    pltpu.make_async_remote_copy(
        tabs.at[pl.ds(0, 3)], tabs.at[pl.ds(0, 3)], tab_send, tab_recv.at[0, 0],
        device_id=device(1, 0, 0, 0), device_id_type=MESH,
    ).wait_send()
    for l in range(LAYERS):
        for s in range(SUBS):
            pltpu.make_async_remote_copy(
                near[l][s], near[l][s], hop_send.at[l, s], hop_recv.at[l, s],
                device_id=device(0, 0, 2, 0), device_id_type=MESH,
            ).wait_send()
            tiles = pl.ds(HERE, 8 * 16 - HERE)
            pltpu.make_async_remote_copy(
                stage.at[l, s, tiles], land[l][s].at[tiles], leaf_send.at[l, s], leaf_recv.at[l, s],
                device_id=device(0, 1, 0, 0), device_id_type=MESH,
            ).wait_send()
    for who in range(PIPE):
        pieces = sum(len(order) for _, _, _, order in acts_of(who))

        @functools.partial(at_y, who)
        def _():
            pltpu.make_async_remote_copy(
                wall.at[:, pl.ds(0, pieces * rows // LAYERS)],
                wall.at[:, pl.ds(0, pieces * rows // LAYERS)],
                w_send, w_recv.at[0, 0],
                device_id=device(1, 0, 0, 0), device_id_type=MESH,
            ).wait_send()


def on_device(features, weights, bias, layout):
    rs = 16 // SUBS
    n = bias.shape[1]
    return pl.pallas_call(
        kernel,
        name="sections",
        out_shape=jax.ShapeDtypeStruct(features.shape, jnp.bfloat16),
        in_specs=[
            pl.BlockSpec(memory_space=pltpu.VMEM),
            pl.BlockSpec(memory_space=pl.ANY),
            pl.BlockSpec(memory_space=pltpu.VMEM),
            pl.BlockSpec(memory_space=pltpu.VMEM),
        ],
        out_specs=pl.BlockSpec(memory_space=pltpu.VMEM),
        scratch_shapes=[
            pltpu.VMEM((LAYERS,) + weights.shape[1:], jnp.bfloat16),
            pltpu.VMEM((LAYERS, BD, 2 * K * BLOCK, 2 * BLOCK), jnp.bfloat16),
            pltpu.VMEM((PIPE, OWN, n), jnp.bfloat16),
            pltpu.VMEM((LAYERS, BD, 2 * BLOCK), jnp.float32),
            pltpu.VMEM((PIPE, OWN, ROWS + 8, 128), jnp.int32),
            pltpu.SMEM((PIPE, OWN, ROWS + 8, 128), jnp.int32),
            [[pltpu.VMEM((BD, rs, 128), jnp.bfloat16)] * SUBS] * LAYERS,
            [[pltpu.VMEM((2, BD, rs, 128), jnp.bfloat16)] * SUBS] * LAYERS,
            pltpu.VMEM((LAYERS, SUBS, 128, rs, 128), jnp.bfloat16),
            [[pltpu.VMEM((128, rs, 128), jnp.bfloat16)] * SUBS] * LAYERS,
            pltpu.SemaphoreType.DMA((1,)),
            pltpu.SemaphoreType.DMA((LAYERS,)),
            pltpu.SemaphoreType.DMA,
            pltpu.SemaphoreType.DMA((PIPE, OWN)),
            pltpu.SemaphoreType.DMA,
            pltpu.SemaphoreType.DMA,
            pltpu.SemaphoreType.DMA,
            pltpu.SemaphoreType.DMA((LAYERS, CHUNKS)),
            pltpu.SemaphoreType.DMA((LAYERS, SUBS)),
            pltpu.SemaphoreType.DMA((LAYERS, SUBS)),
            pltpu.SemaphoreType.DMA((LAYERS, SUBS)),
            pltpu.SemaphoreType.DMA((LAYERS, SUBS)),
        ],
        compiler_params=pltpu.CompilerParams(
            collective_id=0, has_side_effects=True, vmem_limit_bytes=60 * 1024 * 1024
        ),
    )(features, weights, bias, layout)


def solution(mesh):
    in_specs = (
        P("pipe", "rows"),
        P("pipe", "rows", None, None),
        P("pipe", "rows"),
        P("pipe", None),
    )
    return jax.shard_map(
        on_device, mesh=mesh, in_specs=in_specs, out_specs=P("pipe", "rows"), check_vma=False
    )
```

```python
import functools

import jax
import jax.numpy as jnp
from jax import lax
from jax.experimental import pallas as pl
from jax.experimental.pallas import tpu as pltpu
from jax.sharding import PartitionSpec as P

MESH = pl.DeviceIdType.MESH
BLOCK = 64
K = 4
X, Z, C = 4, 8, 2
PIPE = 4
ROWS = X * Z * C
LAYERS = 8
OWN = LAYERS // PIPE
BD = 16
SUBS = 4
CHUNKS = 4
clamp_top = 32.0

OWN_PARTS = ((6, 1, (0,)), (10, -1, (0,)), (0, 0, (0,)))
RELAY_PARTS = ((8, 1, (1,)), (12, -1, (2,)), (2, 0, (1, 2)))
HERE = 6


def place():
    me = lax.axis_index("rows")
    return lax.axis_index("pipe"), me >> 4, (me >> 1) & (Z - 1), me & (C - 1)


def device(dy, dx, dz, dc):
    y, x, z, c = place()
    row = (((x + dx) & (X - 1)) << 4) | (((z + dz) & (Z - 1)) << 1) | ((c ^ dc) & (C - 1))
    return ((y + dy) & (PIPE - 1), row)


def offsets():
    found = [(1, 0, 0, 0), (2, 0, 0, 0), (3, 0, 0, 0), (0, 0, 2, 0), (0, 0, -2, 0)]
    for dx in range(X):
        for dc in range(C):
            for dz in (0, 1, -1, 2 if dc == 0 else -2):
                here = (0, dx, dz, dc)
                if here not in found and here != (0, 0, 0, 0):
                    found.append(here)
    return found


def swap_halves(v):
    return pltpu.roll(v, BLOCK, 1)


def kernel(
    feat_ref, w_hbm, bias_ref, lay_ref, out_ref,
    wall, ready, biases, bias_tiles, tabs, stab, cur, near, stage, land,
    local_sem, smem_sem, tab_send, tab_recv, bias_send, bias_recv, w_send, w_recv,
    hop_send, hop_recv, leaf_send, leaf_recv,
):
    y, x, z, c = place()
    me = (x * Z + z) * C + c
    rs = cur[0][0].shape[1]
    left = lax.broadcasted_iota(jnp.int32, (BD, 128), 1) < BLOCK

    barrier = pltpu.get_barrier_semaphore()
    partners = offsets()
    for dy, dx, dz, dc in partners:
        pl.semaphore_signal(
            barrier, inc=1, device_id=device(-dy, -dx, -dz, -dc), device_id_type=MESH
        )

    own_w = pltpu.make_async_copy(w_hbm, wall.at[pl.ds(OWN * y, OWN)], local_sem.at[0])
    own_w.start()

    def fold(p, carry):
        cols = pl.ds(pl.multiple_of(p * 128, 128), 128)
        low = feat_ref[pl.ds(0, 16), cols].astype(jnp.float32)
        high = feat_ref[pl.ds(16, 16), cols].astype(jnp.float32)
        even = jnp.where(left, low, swap_halves(high)).astype(jnp.bfloat16)
        odd = jnp.where(left, swap_halves(low), high).astype(jnp.bfloat16)
        for s in range(SUBS):
            cur[0][s][2 * p] = even[s * rs : (s + 1) * rs]
            cur[0][s][2 * p + 1] = odd[s * rs : (s + 1) * rs]
        return carry

    lax.fori_loop(0, BD // 2, fold, 0)
    biases[pl.ds(y, 1)] = bias_ref[...].reshape(1, OWN, bias_ref.shape[1])

    lane = lax.broadcasted_iota(jnp.int32, (ROWS // 2, 128), 1)
    slot = lane & 63
    for a in range(OWN):
        entry = jnp.concatenate(
            [lay_ref[pl.ds(a, 1), pl.ds(i * 128, 128)] for i in range(ROWS // 2)], axis=0
        )
        owner = entry >> 4
        key = slot * BD + (entry & 15)
        for half in range(2):
            table = jnp.zeros((ROWS // 2, 128), jnp.int32)
            for q, dz in enumerate((0, -2, 2)):
                source = (x << 4) | (((z + dz) & (Z - 1)) << 1) | c
                hit = (owner == source) & ((lane >> 6) == half)
                first = jnp.min(jnp.where(hit, key, 1 << 20), axis=1, keepdims=True) & 15
                last = jnp.max(jnp.where(hit, key, 0), axis=1, keepdims=True) & 15
                table = jnp.where(lane == 2 * q, first, table)
                table = jnp.where(lane == 2 * q + 1, last, table)
            tabs[y, a, pl.ds(half * ROWS // 2, ROWS // 2)] = table
    mine = jnp.concatenate(
        [lay_ref[:, pl.ds(pl.multiple_of((x * Z + z) * 128, 128), 128)]]
        + [jnp.zeros((8 - OWN, 128), jnp.int32)],
        axis=0,
    )
    owner = mine >> 4
    spot = lax.broadcasted_iota(jnp.int32, (8, 128), 1) & 63
    rank = jnp.zeros((8, 128), jnp.int32)
    for step in range(1, 64):
        same = (pltpu.roll(owner, step, 1) == owner) & (spot >= step)
        rank = jnp.where(same, 1, rank)
    dx = (x - (owner >> 4) + X) & (X - 1)
    dz = (z - ((owner >> 1) & (Z - 1)) + Z) & (Z - 1)
    dc = (c + owner) & 1
    base = jnp.zeros((8, 128), jnp.int32)
    for d, at in ((0, 0), (2, 2), (6, 4), (1, 6), (3, 8), (7, 10), (5, 12), (4, 14)):
        base = jnp.where(dz == d, at, base)
    where = (dx * 2 + dc) * 16 + base + rank
    for a in range(OWN):
        both_rows = jnp.concatenate(
            [where[a : a + 1], pltpu.roll(where, 64, 1)[a : a + 1], jnp.zeros((6, 128), jnp.int32)], axis=0
        )
        tabs[y, a, pl.ds(ROWS, 8)] = both_rows

    own_w.wait()
    with jax.named_scope("barrier_wait"):
        pl.semaphore_wait(barrier, len(partners))

    def tab_copy(a, dy):
        return pltpu.make_async_remote_copy(
            tabs.at[y, a], tabs.at[y, a], tab_send, tab_recv.at[y, a],
            device_id=device(dy, 0, 0, 0), device_id_type=MESH,
        )

    def bias_copy(dy):
        return pltpu.make_async_remote_copy(
            biases.at[y], biases.at[y], bias_send, bias_recv,
            device_id=device(dy, 0, 0, 0), device_id_type=MESH,
        )

    def hop(l, s, dz, q):
        return pltpu.make_async_remote_copy(
            cur[l][s], near[l][s].at[q], hop_send.at[l, s], hop_recv.at[l, s],
            device_id=device(0, 0, dz, 0), device_id_type=MESH,
        )

    def start_hops(l, s):
        hop(l, s, 2, 0).start()
        hop(l, s, -2, 1).start()

    rows = BD // CHUNKS

    def w_copy(l, chunk, dy, src):
        piece = pl.ds(chunk * rows, rows)
        return pltpu.make_async_remote_copy(
            src.at[piece], wall.at[l, piece], w_send, w_recv.at[l, chunk],
            device_id=device(dy, 0, 0, 0), device_id_type=MESH,
        )

    def w_own(a, dy, order):
        for chunk in order:
            w_copy(OWN * y + a, chunk, dy, wall.at[OWN * y + a]).start()

    def w_wait(l, order):
        for chunk in order:
            w_copy(l, chunk, 1, wall.at[l]).wait_recv()

    def w_pass(l, order, dy):
        for chunk in order:
            w_wait(l, (chunk,))
            w_copy(l, chunk, dy, wall.at[l]).start()

    def at_y(which, act):
        pl.when(y == which)(act)


    h1, h2 = (0, 1), (2, 3)

    def own(which, *ways):
        return tuple(
            ("own", which, dy, chunks or (h1 + h2 if dy > 0 else h2 + h1)) for dy, chunks in ways
        )

    def fwd(l, dy, chunks):
        return (("pass", l, dy, chunks),)

    up, down = (1, None), (-1, None)
    program = {
        "start": (
            (0, own(0, up, down)),
            (1, own(0, down) + own(1, down)),
            (2, own(0, down) + own(1, down)),
            (3, own(0, up) + own(1, up)),
        ),
        "first": (
            (0, own(1, up, down)),
            (1, fwd(0, 1, h1) + own(0, (1, h1))),
            (3, fwd(0, -1, h2)),
        ),
        (0, 0): ((1, fwd(1, 1, (0,))), (3, fwd(1, -1, (2,)))),
        (0, 1): (
            (1, fwd(1, 1, (1,)) + own(0, (1, h2)) + own(1, up)),
            (3, fwd(1, -1, (3,)) + own(0, down) + own(1, down)),
        ),
        (0, 2): ((2, fwd(2, 1, h1) + own(0, (1, h1))),),
        (0, 3): ((0, fwd(2, -1, h2)),),
        (1, 0): ((0, fwd(3, -1, h2)), (1, fwd(4, -1, h1 + h2) + fwd(5, -1, h1 + h2))),
        (1, 3): ((2, fwd(3, 1, (0,))),),
        (2, 0): ((2, fwd(3, 1, (1,)) + own(0, (1, h2))),),
        (2, 1): ((0, fwd(6, 1, h1) + fwd(7, 1, h1)), (2, own(1, up) + fwd(6, -1, h2))),
        (3, 0): ((2, fwd(7, -1, h2)),),
    }

    def acts_of(who):
        return [act for step in program.values() for y_at, acts in step if y_at == who for act in acts]

    def point(*at):
        for who, acts in program.get(at if len(at) > 1 else at[0], ()):
            @functools.partial(at_y, who)
            def _():
                for kind, which, dy, order in acts:
                    if kind == "own":
                        w_own(which, dy, order)
                    else:
                        w_pass(which, order, dy)

    def arrive(l):
        owner = l // OWN
        for who in range(PIPE):
            passed = [
                chunk
                for kind, which, _, order in acts_of(who) if kind == "pass" and which == l
                for chunk in order
            ]
            order = tuple(chunk for chunk in h1 + h2 if chunk not in passed)
            if who != owner and order:
                at_y(who, functools.partial(w_wait, l, order))

    def prepare(l):
        keep = lax.broadcasted_iota(jnp.int32, (BLOCK, 128), 1) < BLOCK

        def one(r, carry):
            for p in range(2):
                raw = wall[l, r, :, pl.ds(p * 128, 128)].astype(jnp.float32)
                turn = swap_halves(raw)
                zero = jnp.zeros_like(raw)
                parts = (
                    jnp.where(keep, raw, zero), jnp.where(keep, zero, turn),
                    jnp.where(keep, turn, zero), jnp.where(keep, zero, raw),
                )
                for i, part in enumerate(parts):
                    ready[l, r, pl.ds((p * 4 + i) * BLOCK, BLOCK), :] = part.astype(jnp.bfloat16)
            return carry

        lax.fori_loop(0, BD, one, 0, unroll=4)

        line_left = lax.broadcasted_iota(jnp.int32, (1, 128), 1) < BLOCK

        for p in range(BD // 2):
            row = biases[l // OWN, pl.ds(l % OWN, 1), pl.ds(p * 128, 128)].astype(jnp.float32)
            turn = swap_halves(row)
            bias_tiles[l, pl.ds(2 * p, 1), :] = jnp.where(line_left, row, turn)
            bias_tiles[l, pl.ds(2 * p + 1, 1), :] = jnp.where(line_left, turn, row)

    def leaf(l, s, base, dx, dz, dc, at, n):
        tiles = pl.ds(base + at, n)
        return pltpu.make_async_remote_copy(
            stage.at[l, s, tiles], land[l][s].at[tiles], leaf_send.at[l, s], leaf_recv.at[l, s],
            device_id=device(0, dx, dz, dc), device_id_type=MESH,
        )

    def hop_wait(l, s):
        pltpu.make_async_remote_copy(
            near[l][s], near[l][s], hop_send.at[l, s], hop_recv.at[l, s],
            device_id=device(0, 0, 2, 0), device_id_type=MESH,
        ).wait_recv()

    def columns(l, s, parts, relay, far):
        def column(t, carry):
            dx = t ^ 2
            xx = ((x + dx) & (X - 1)) << 3
            plans = []
            for dc in range(C):
                todo = parts
                if far:
                    todo = ((14, 2 - 4 * dc, (1 + dc,)),) + parts
                plans.append((dc, (dx * 2 + dc) * 16, todo))
            moves = []
            for dc, base, todo in plans:
                for at, dz, sources in todo:
                    row = ((c ^ dc) << 5) | xx | ((z + dz) & (Z - 1))
                    for i, q in enumerate(sources):
                        for k in range(2):
                            index = stab[l // OWN, l % OWN, row, 2 * q + k]
                            moves.append((base + at + 2 * i + k, q, index))
            tiles = [near[l][s][q - 1, i] if relay else cur[l][s][i] for _, q, i in moves]
            for (at, _, _), tile in zip(moves, tiles):
                stage[l, s, at] = tile
            for dc, base, todo in plans:
                for at, dz, sources in todo:
                    go = leaf(l, s, base, dx, dz, dc, at, 2 * len(sources))
                    if dz == 0 and dc == 0:
                        pl.when(dx > 0)(go.start)
                    else:
                        go.start()
            return carry

        lax.fori_loop(0, X, column, 0)
        for at, dz, sources in parts:
            if dz == 0:
                for k in range(at, at + 2 * len(sources)):
                    land[l][s][k] = stage[l, s, k]

    def pack_own(l, s):
        columns(l, s, OWN_PARTS, False, False)

    def pack(l, s):
        columns(l, s, RELAY_PARTS[:2], True, True)
        columns(l, s, RELAY_PARTS[2:], True, False)

    def spread(l, s):
        hop_wait(l, s)
        pack(l, s)

    def gather(l, s):
        tiles = pl.ds(HERE, 8 * 16 - HERE)
        pltpu.make_async_remote_copy(
            stage.at[l, s, tiles], land[l][s].at[tiles], leaf_send.at[l, s], leaf_recv.at[l, s],
            device_id=device(0, 1, 0, 0), device_id_type=MESH,
        ).wait_recv()

    def block_out(l, s, r):
        row = stab.at[l // OWN, l % OWN, ROWS + c]
        lhs = jnp.concatenate([land[l][s][row[r * K + k]] for k in range(K)], axis=1)
        total = jnp.dot(lhs, ready[l, r], preferred_element_type=jnp.float32)
        total = total + bias_tiles[l, pl.ds(r, 1), :]
        return jnp.minimum(jnp.maximum(total, 0.0), clamp_top)

    def advance(l, s):
        gather(l, s)
        compute(l, s)
        start_hops(l + 1, s)
        pack_own(l + 1, s)

    def compute(l, s):
        def pair(p, carry):
            for r in range(2):
                cur[l + 1][s][2 * p + r] = block_out(l, s, 2 * p + r).astype(jnp.bfloat16)
            return carry

        lax.fori_loop(0, BD // 2, pair, 0, unroll=8)

    def finish(l, s):
        gather(l, s)
        finish_compute(l, s)

    def finish_compute(l, s):
        half = left[:rs]

        def pair(p, carry):
            even, odd = block_out(l, s, 2 * p), block_out(l, s, 2 * p + 1)
            cols = pl.ds(pl.multiple_of(p * 128, 128), 128)
            low = jnp.where(half, even, swap_halves(odd))
            high = jnp.where(half, swap_halves(even), odd)
            out_ref[pl.ds(s * rs, rs), cols] = low.astype(jnp.bfloat16)
            out_ref[pl.ds(16 + s * rs, rs), cols] = high.astype(jnp.bfloat16)
            return carry

        lax.fori_loop(0, BD // 2, pair, 0, unroll=8)

    def tab_wait(l):
        @pl.when(y != l // OWN)
        def _():
            at = (l // OWN, l % OWN)
            pltpu.make_async_remote_copy(
                tabs.at[at], tabs.at[at], tab_send, tab_recv.at[at],
                device_id=device(1, 0, 0, 0), device_id_type=MESH,
            ).wait_recv()

    def to_smem(l):
        at = (l // OWN, l % OWN)
        return pltpu.make_async_copy(tabs.at[at], stab.at[at], smem_sem.at[l])

    def smem_wait(l):
        to_smem(l).wait()

    for dy in (2, 1, 3):
        tab_copy(0, dy).start()
    for s in range(SUBS):
        start_hops(0, s)
    for dy in (2, 1, 3):
        tab_copy(1, dy).start()
    for dy in (1, 2, 3):
        bias_copy(dy).start()
    point("start")
    tab_wait(0)
    to_smem(0).start()
    smem_wait(0)
    for s in range(SUBS):
        pack_own(0, s)
    for s in range(SUBS):
        spread(0, s)
    for l in range(1, LAYERS):
        tab_wait(l)
        to_smem(l).start()
    pltpu.make_async_remote_copy(
        biases.at[pl.ds(0, 3)], biases.at[pl.ds(0, 3)], bias_send, bias_recv,
        device_id=device(1, 0, 0, 0), device_id_type=MESH,
    ).wait()
    point("first")
    arrive(0)
    prepare(0)
    last = LAYERS - 1
    for l in range(LAYERS):
        if l == last:
            for s in range(SUBS):
                finish(l, s)
            break
        smem_wait(l + 1)
        for s in range(SUBS):
            advance(l, s)
        point(l, 0)
        point(l, 1)
        for s in range(SUBS):
            spread(l + 1, s)
        point(l, 2)
        point(l, 3)
        arrive(l + 1)
        prepare(l + 1)

    pltpu.make_async_remote_copy(
        tabs.at[pl.ds(0, 3)], tabs.at[pl.ds(0, 3)], tab_send, tab_recv.at[0, 0],
        device_id=device(1, 0, 0, 0), device_id_type=MESH,
    ).wait_send()
    for l in range(LAYERS):
        for s in range(SUBS):
            pltpu.make_async_remote_copy(
                near[l][s], near[l][s], hop_send.at[l, s], hop_recv.at[l, s],
                device_id=device(0, 0, 2, 0), device_id_type=MESH,
            ).wait_send()
            tiles = pl.ds(HERE, 8 * 16 - HERE)
            pltpu.make_async_remote_copy(
                stage.at[l, s, tiles], land[l][s].at[tiles], leaf_send.at[l, s], leaf_recv.at[l, s],
                device_id=device(0, 1, 0, 0), device_id_type=MESH,
            ).wait_send()
    for who in range(PIPE):
        pieces = sum(len(order) for _, _, _, order in acts_of(who))

        @functools.partial(at_y, who)
        def _():
            pltpu.make_async_remote_copy(
                wall.at[:, pl.ds(0, pieces * rows // LAYERS)],
                wall.at[:, pl.ds(0, pieces * rows // LAYERS)],
                w_send, w_recv.at[0, 0],
                device_id=device(1, 0, 0, 0), device_id_type=MESH,
            ).wait_send()


def on_device(features, weights, bias, layout):
    rs = 16 // SUBS
    n = bias.shape[1]
    return pl.pallas_call(
        kernel,
        name="sections",
        out_shape=jax.ShapeDtypeStruct(features.shape, jnp.bfloat16),
        in_specs=[
            pl.BlockSpec(memory_space=pltpu.VMEM),
            pl.BlockSpec(memory_space=pl.ANY),
            pl.BlockSpec(memory_space=pltpu.VMEM),
            pl.BlockSpec(memory_space=pltpu.VMEM),
        ],
        out_specs=pl.BlockSpec(memory_space=pltpu.VMEM),
        scratch_shapes=[
            pltpu.VMEM((LAYERS,) + weights.shape[1:], jnp.bfloat16),
            pltpu.VMEM((LAYERS, BD, 2 * K * BLOCK, 2 * BLOCK), jnp.bfloat16),
            pltpu.VMEM((PIPE, OWN, n), jnp.bfloat16),
            pltpu.VMEM((LAYERS, BD, 2 * BLOCK), jnp.float32),
            pltpu.VMEM((PIPE, OWN, ROWS + 8, 128), jnp.int32),
            pltpu.SMEM((PIPE, OWN, ROWS + 8, 128), jnp.int32),
            [[pltpu.VMEM((BD, rs, 128), jnp.bfloat16)] * SUBS] * LAYERS,
            [[pltpu.VMEM((2, BD, rs, 128), jnp.bfloat16)] * SUBS] * LAYERS,
            pltpu.VMEM((LAYERS, SUBS, 128, rs, 128), jnp.bfloat16),
            [[pltpu.VMEM((128, rs, 128), jnp.bfloat16)] * SUBS] * LAYERS,
            pltpu.SemaphoreType.DMA((1,)),
            pltpu.SemaphoreType.DMA((LAYERS,)),
            pltpu.SemaphoreType.DMA,
            pltpu.SemaphoreType.DMA((PIPE, OWN)),
            pltpu.SemaphoreType.DMA,
            pltpu.SemaphoreType.DMA,
            pltpu.SemaphoreType.DMA,
            pltpu.SemaphoreType.DMA((LAYERS, CHUNKS)),
            pltpu.SemaphoreType.DMA((LAYERS, SUBS)),
            pltpu.SemaphoreType.DMA((LAYERS, SUBS)),
            pltpu.SemaphoreType.DMA((LAYERS, SUBS)),
            pltpu.SemaphoreType.DMA((LAYERS, SUBS)),
        ],
        compiler_params=pltpu.CompilerParams(
            collective_id=0, has_side_effects=True, vmem_limit_bytes=60 * 1024 * 1024
        ),
    )(features, weights, bias, layout)


def solution(mesh):
    in_specs = (
        P("pipe", "rows"),
        P("pipe", "rows", None, None),
        P("pipe", "rows"),
        P("pipe", None),
    )
    return jax.shard_map(
        on_device, mesh=mesh, in_specs=in_specs, out_specs=P("pipe", "rows"), check_vma=False
    )
```
